32 devices in a mesh: line: 16 (over z, y, x), sec: 2 (over core).
Axes of the slice: x: 2, y: 2, z: 4, core: 2. Of those that a mesh axis runs over, the one named last changes fastest.
Arguments:
- right_side: float32 [16, 2, 256, 256], P('line', 'sec'), may hold values from -80 to 80
- inverse_diag: float32 [16, 2, 256, 256], P('line', 'sec'), may hold values from -3 to 3
- couplings: float32 [16, 2, 2, 256, 256], P('line', 'sec'), may hold values from -0.5 to 0.5
- neighbors: int32 [16, 2, 2], P('line', 'sec'), may hold values from -1 to 0, as said below
Outputs:
- panel: float32 [16, 2, 256, 256], P('line', 'sec')
- factor: float32 [256, 256], replicated
The draws below stay inside these ranges and needn't reach their ends.
Inputs may be any that keep to these rules, and one draw needn't show every extreme that they name: `neighbors`: every entry is -1 or a section lower than its own; slot 0 of every section after the first names the section just before it; the first section's entries are all -1.
All inputs are finite; a program needn't handle non-finite values.
Results may differ from the reference program's by a relative error of at most 0.0001.
Values sent between devices are 32-bit elements; how exact they have to be, the bound alone decides.
No kernel may reach another device: no remote copies, remote signals or barrier semaphores. Data moves between devices by JAX's collectives and lax.ppermute only.
A program may use at most 64 MiB of HBM per device.

```python
import jax
import jax.numpy as jnp
from jax import lax

ROWS = 256
WIDTH = 256
NB = 2
LINES = 16
SECS = 2
NTOT = 8192


def draw_right_side(key, part):
    line_pos = jnp.arange(LINES, dtype=jnp.float32)[:, None] / max(LINES - 1, 1)
    sec_pos = jnp.arange(SECS, dtype=jnp.float32)[None, :] / max(SECS - 1, 1)
    factor = jax.random.uniform(jax.random.fold_in(key, 1), (LINES, SECS), jnp.float32, 1.0, 2.0)
    scale = jnp.exp(jnp.log(3.0) * (line_pos + sec_pos)) * factor
    base = jnp.clip(jax.random.normal(jax.random.fold_in(key, 2), (LINES, SECS, ROWS, WIDTH), jnp.float32), -4.0, 4.0)
    return base * scale[:, :, None, None]


def draw_inverse_diag(key, part):
    spread = 0.35 / ROWS ** 0.5
    off = jnp.clip(jax.random.normal(jax.random.fold_in(key, 4), (LINES, SECS, ROWS, ROWS), jnp.float32), -4.0, 4.0) * spread
    diag = jnp.exp(jax.random.uniform(jax.random.fold_in(key, 5), (LINES, SECS, ROWS), jnp.float32, 0.0, jnp.log(2.0)))
    return off + diag[..., None] * jnp.eye(ROWS, dtype=jnp.float32)


def draw_neighbors(key, part):
    section = jnp.arange(SECS, dtype=jnp.int32)[None, :, None]
    bits = jax.random.randint(jax.random.fold_in(key, 6), (LINES, SECS, NB), 0, 1 << 20)
    slot = jnp.arange(NB, dtype=jnp.int32)[None, None, :]
    other = bits % (section + 1) - 1
    picked = jnp.where(slot == 0, section - 1, other)
    return jnp.where(section == 0, -1, picked).astype(jnp.int32)


def levels(rng, dims, cuts, smallest, top_value):
    loudness, own = 1.0, jax.random.fold_in(rng, 6)
    for position, shards_of in cuts:
        steps = jnp.exp(jax.random.uniform(jax.random.fold_in(own, position), (shards_of,), jnp.float32, smallest / len(cuts), top_value / len(cuts)))
        loudness = loudness * jnp.repeat(steps, dims[position] // shards_of).reshape([-1 if axis == position else 1 for axis in range(len(dims))])
    return loudness


def bell_draw(rng, extent, scale, reach, pieces=(), kind=jnp.bfloat16):
    result = scale * jax.random.normal(rng, extent, jnp.float32)
    if pieces:
        result = result * levels(rng, extent, pieces, -0.22, 0.18)
    return jnp.clip(result, -reach, reach).astype(kind)


def setup_inputs(seed: int = 0) -> dict:
    key_list = jax.random.split(jax.random.key(seed), 5)
    right_side = draw_right_side(jax.random.fold_in(key_list[4], 71), 0)
    inverse_diag = draw_inverse_diag(jax.random.fold_in(key_list[4], 71), 0)
    couplings = bell_draw(key_list[2], (LINES, SECS, NB, ROWS, ROWS), (0.5 * ROWS ** -0.5), 0.5, ((0, 16), (1, 2)), jnp.float32)
    neighbors = draw_neighbors(jax.random.fold_in(key_list[4], 71), 0)
    return dict(right_side=right_side, inverse_diag=inverse_diag, couplings=couplings, neighbors=neighbors)


def reference(right_side, inverse_diag, couplings, neighbors):
    solved = jnp.zeros_like(right_side)
    for section in range(SECS):
        acc = right_side[:, section]
        for slot in range(NB):
            index = neighbors[:, section, slot]
            safe = jnp.maximum(index, 0).astype(jnp.int32)
            picked = jnp.take_along_axis(solved, safe[:, None, None, None], axis=1)[:, 0]
            term = jnp.einsum('lij,ljw->liw', couplings[:, section, slot], picked, precision=lax.Precision.HIGHEST)
            acc = acc - jnp.where((index >= 0)[:, None, None], term, jnp.float32(0.0))
        block = jnp.einsum('lij,ljw->liw', inverse_diag[:, section], acc, precision=lax.Precision.HIGHEST)
        solved = solved.at[:, section].set(block)
    matrix = solved.reshape(LINES * SECS * ROWS, WIDTH)
    gram = jnp.dot(matrix.T.astype(jnp.float32), matrix.astype(jnp.float32), precision=lax.Precision.HIGHEST, preferred_element_type=jnp.float32) / NTOT
    lower = jnp.linalg.cholesky(gram)
    normed = jax.scipy.linalg.solve_triangular(lower, matrix.T, lower=True).T
    return (normed.reshape(LINES, SECS, ROWS, WIDTH), lower.T)
```

```python
import functools

import jax
import jax.numpy as jnp
from jax import lax
from jax.experimental import pallas as pl
from jax.experimental.pallas import tpu as pltpu
from jax.sharding import PartitionSpec as P


AXES = ("line", "sec")
VMEM = pl.BlockSpec(memory_space=pltpu.VMEM)
SMEM = pl.BlockSpec(memory_space=pltpu.SMEM)
NN = (((1,), (0,)), ((), ()))
NT = (((1,), (1,)), ((), ()))
TN = (((0,), (0,)), ((), ()))


def exact(left, right, dims=NN):
    return lax.dot_general(
        left, right, dims, precision=lax.Precision.HIGHEST, preferred_element_type=jnp.float32
    )


def coarse(left, right, dims=NN):
    return lax.dot_general(
        left.astype(jnp.bfloat16),
        right.astype(jnp.bfloat16),
        dims,
        preferred_element_type=jnp.float32,
    )


def split(value):
    high = value.astype(jnp.bfloat16)
    return high, (value - high.astype(jnp.float32)).astype(jnp.bfloat16)


def middle(left, right, dims=NN):
    (lh, ll), (rh, rl) = split(left), split(right)
    dot = functools.partial(
        lax.dot_general, dimension_numbers=dims, preferred_element_type=jnp.float32
    )
    return dot(lh, rh) + (dot(lh, rl) + dot(ll, rh))


def call(kernel, outs, specs, name, flops, scratch=()):
    moved = sum(4 * out.size for out in outs)
    return pl.pallas_call(
        kernel,
        out_shape=outs,
        in_specs=specs,
        out_specs=[VMEM] * len(outs),
        scratch_shapes=list(scratch),
        compiler_params=pltpu.CompilerParams(vmem_limit_bytes=16 << 20),
        cost_estimate=pl.CostEstimate(flops=flops, bytes_accessed=moved, transcendentals=0),
        name=name,
    )


def shape(*dims):
    return jax.ShapeDtypeStruct(dims, jnp.float32)


def grids(rows, cols):
    return (
        lax.broadcasted_iota(jnp.int32, (rows, cols), 0),
        lax.broadcasted_iota(jnp.int32, (rows, cols), 1),
    )


def front_kernel(links, target, inverse, coupled, out):
    rows = target.shape[0]
    matrix = jnp.zeros(inverse.shape, jnp.float32)
    for slot in range(coupled.shape[0]):
        matrix = matrix + jnp.where(links[slot] >= 0, coupled[slot], 0.0)
    out[:rows, :] = exact(inverse[...], target[...])
    out[rows:, :] = exact(inverse[...], matrix)


def packed(gram, half):
    i, j = grids(half, half)
    last = gram[half:, half:]
    corner = jnp.where(i >= j, gram[:half, :half], last)
    diagonal = jnp.sum(jnp.where(i == j, last, 0.0), axis=0, keepdims=True)
    return gram[half:, :half], corner, diagonal


def gram_kernel(scale, place, own, other, solved, piece):
    rows = own.shape[0] // 2
    half = own.shape[1] // 2
    lead = place[0] == 0
    first = jnp.where(lead, own[:rows, :], other[:rows, :])
    base = jnp.where(lead, other[:rows, :], own[:rows, :])
    carry = jnp.where(lead, other[rows:, :], own[rows:, :])
    second = base - exact(carry, first)
    solved[...] = jnp.where(lead, first, second)
    gram = (exact(first, first, TN) + exact(second, second, TN)) * scale
    block, corner, diagonal = packed(gram, half)
    piece[:half, :] = jnp.where(lead, block, corner)
    piece[half:, :] = jnp.broadcast_to(diagonal, (piece.shape[0] - half, half))


def eliminate(gram, inverse, factor):
    size = gram.shape[0]
    i, j = grids(size, size)
    inverse[...] = jnp.where(i == j, 1.0, 0.0)
    factor[...] = jnp.zeros_like(factor)
    lane = lax.broadcasted_iota(jnp.int32, (1, size), 1)
    line = lax.broadcasted_iota(jnp.int32, (size, 1), 0)

    def step(k, carry):
        matrix = gram[...]
        pivot = jnp.sum(jnp.where((i == k) & (j == k), matrix, 0.0), axis=(0, 1), keepdims=True)
        root = lax.rsqrt(pivot)
        root = root * (1.5 - 0.5 * pivot * root * root)
        column = jnp.sum(jnp.where(j == k, matrix, 0.0), axis=1, keepdims=True) * root
        row = jnp.sum(jnp.where(i == k, matrix, 0.0), axis=0, keepdims=True) * root
        row = jnp.where(lane >= k, row, 0.0)
        column = jnp.where(line > k, column, 0.0)
        lead = jnp.sum(jnp.where(i == k, inverse[...], 0.0), axis=0, keepdims=True) * root
        gram[...] = matrix - column * row
        inverse[...] = jnp.where(i == k, lead, inverse[...] - column * lead)
        factor[...] = jnp.where(i == k, row, factor[...])
        return carry

    lax.fori_loop(0, size, step, 0)


def improved(error, weight, dot):
    lower = error * weight
    return weight * dot(lower, lower, NT) + (dot(lower, lower) - lower)


def factor_kernel(place, mine, theirs, solved, panel, factor, gram_ref, inverse_ref, factor_ref):
    half = mine.shape[1]
    size = 2 * half
    lead = place[0] == 0
    block = jnp.where(lead, mine[:half, :], theirs[:half, :])
    corner = jnp.where(lead, theirs[:half, :], mine[:half, :])
    diagonal = jnp.where(lead, theirs[half : half + 1, :], mine[half : half + 1, :])
    i, j = grids(half, half)
    mirrored = corner.T
    gram_ref[:half, :half] = jnp.where(i >= j, corner, mirrored)
    gram_ref[half:, half:] = jnp.where(i < j, corner, jnp.where(i == j, diagonal, mirrored))
    gram_ref[half:, :half] = block
    gram_ref[:half, half:] = block.T
    gram = gram_ref[...]

    i, j = grids(size, size)
    unit = jnp.where(i == j, 1.0, 0.0)
    weight = jnp.where(i > j, 1.0, jnp.where(i == j, 0.5, 0.0))
    spread = gram * unit
    row = lax.rsqrt(jnp.sum(spread, axis=0, keepdims=True))
    column = lax.rsqrt(jnp.sum(spread, axis=1, keepdims=True))
    scaled = gram * column * row
    step = improved(scaled - unit, weight, coarse)
    trial = unit + step
    product = coarse(trial, scaled)
    error = coarse(product, trial, NT) - unit
    trial = trial + coarse(improved(error, weight, coarse), trial)
    product = exact(trial, scaled)
    error = exact(product, trial, NT) - unit
    step = improved(error, weight, coarse)
    near = exact(solved[...] * row, trial, NT)
    panel[...] = near + middle(near, step, NT)
    upper = product + middle(step, product)
    factor[...] = jnp.where(i <= j, upper / row, 0.0)
    settled = jnp.max(jnp.abs(error)) < 0.02

    @pl.when(jnp.logical_not(settled))
    def _():
        eliminate(gram_ref, inverse_ref, factor_ref)
        panel[...] = exact(solved[...], inverse_ref[...], NT)
        factor[...] = factor_ref[...]


def finish(place, mine, theirs, solved):
    rows, size = solved.shape
    scratch = [pltpu.VMEM((size, size), jnp.float32)] * 3
    return call(
        factor_kernel,
        [shape(rows, size), shape(size, size)],
        [SMEM, VMEM, VMEM, VMEM],
        "factor",
        24 * 2 * size**3,
        scratch,
    )(place, mine, theirs, solved)


def swap_lines(piece, lines):
    bits = [1 << b for b in range((lines - 1).bit_length())]
    other = [bits[b ^ 1] if b ^ 1 < len(bits) else bits[b] for b in range(len(bits))]
    for even, odd in zip(bits, other):
        pairs = []
        for line in range(lines):
            pairs.append((2 * line, 2 * (line ^ even)))
            pairs.append((2 * line + 1, 2 * (line ^ odd) + 1))
        piece = piece + lax.ppermute(piece, AXES, pairs)
    return piece


def two_sections(target, inverse, coupled, links, lines):
    rows, width = target.shape
    half = width // 2
    place = jnp.reshape(lax.axis_index("sec"), (1,))
    own = call(
        front_kernel,
        [shape(rows + inverse.shape[0], width)],
        [SMEM, VMEM, VMEM, VMEM],
        "front",
        4 * rows * rows * width,
    )(links, target, inverse, coupled)[0]
    swap = [(0, 1), (1, 0)]
    other = lax.ppermute(own, "sec", swap)
    scale = 1.0 / (2 * lines * rows)
    solved, piece = call(
        functools.partial(gram_kernel, scale),
        [shape(rows, width), shape(half + 8, half)],
        [SMEM, VMEM, VMEM],
        "gram",
        6 * rows * rows * width,
    )(place, own, other)
    piece = swap_lines(piece, lines)
    theirs = lax.ppermute(piece, "sec", swap)
    return finish(place, piece, theirs, solved)


def many_sections(target, inverse, coupled, links):
    section = lax.axis_index("sec")
    count = lax.axis_size("sec")
    acc = target
    solved = jnp.zeros_like(target)
    for anchor in range(count):
        mine = section == anchor
        candidate = jnp.where(mine, exact(inverse, acc), 0.0)
        arrived = lax.psum(candidate, "sec")
        solved = jnp.where(mine, arrived, solved)
        matrix = jnp.zeros_like(inverse)
        for slot in range(coupled.shape[0]):
            matrix = matrix + jnp.where(links[slot] == anchor, coupled[slot], 0.0)
        acc = acc - exact(matrix, arrived)
    total = lax.axis_size("line") * count * target.shape[0]
    gram = lax.psum(exact(solved, solved, TN), AXES) / total
    half = target.shape[1] // 2
    block, corner, diagonal = packed(gram, half)
    rest = jnp.broadcast_to(diagonal, (8, half))
    place = jnp.zeros((1,), jnp.int32)
    return finish(
        place, jnp.concatenate([block, rest]), jnp.concatenate([corner, rest]), solved
    )


def shards(right_side, inverse_diag, couplings, neighbors):
    local = (right_side[0, 0], inverse_diag[0, 0], couplings[0, 0], neighbors[0, 0])
    lines = lax.axis_size("line")
    if lax.axis_size("sec") == 2 and lines & (lines - 1) == 0:
        panel, factor = two_sections(*local, lines)
    else:
        panel, factor = many_sections(*local)
    return (panel[None, None], factor)


def solution(mesh):
    placed = (
        P("line", "sec", None, None),
        P("line", "sec", None, None),
        P("line", "sec", None, None, None),
        P("line", "sec", None),
    )
    return jax.shard_map(
        shards,
        mesh=mesh,
        in_specs=placed,
        out_specs=(P("line", "sec", None, None), P()),
        check_vma=False,
    )
```

```python
import functools

import jax
import jax.numpy as jnp
from jax import lax
from jax.experimental import pallas as pl
from jax.experimental.pallas import tpu as pltpu
from jax.sharding import PartitionSpec as P


AXES = ("line", "sec")
VMEM = pl.BlockSpec(memory_space=pltpu.VMEM)
HBM = pl.BlockSpec(memory_space=pltpu.HBM)
NN = (((1,), (0,)), ((), ()))
NT = (((1,), (1,)), ((), ()))
TN = (((0,), (0,)), ((), ()))


def exact(left, right, dims=NN):
    return lax.dot_general(
        left, right, dims, precision=lax.Precision.HIGHEST, preferred_element_type=jnp.float32
    )


def coarse(left, right, dims=NN):
    return lax.dot_general(
        left.astype(jnp.bfloat16),
        right.astype(jnp.bfloat16),
        dims,
        preferred_element_type=jnp.float32,
    )


def split(value):
    high = value.astype(jnp.bfloat16)
    return high, (value - high.astype(jnp.float32)).astype(jnp.bfloat16)


def middle(left, right, dims=NN):
    (lh, ll), (rh, rl) = split(left), split(right)
    dot = functools.partial(
        lax.dot_general, dimension_numbers=dims, preferred_element_type=jnp.float32
    )
    return dot(lh, rh) + (dot(lh, rl) + dot(ll, rh))


def call(kernel, outs, specs, name, flops, scratch=()):
    moved = sum(4 * out.size for out in outs)
    return pl.pallas_call(
        kernel,
        out_shape=outs,
        in_specs=specs,
        out_specs=[VMEM] * len(outs),
        scratch_shapes=list(scratch),
        compiler_params=pltpu.CompilerParams(vmem_limit_bytes=16 << 20),
        cost_estimate=pl.CostEstimate(flops=flops, bytes_accessed=moved, transcendentals=0),
        name=name,
    )


def fetched(value):
    return pltpu.with_memory_space_constraint(value, pltpu.HBM)


def shape(*dims):
    return jax.ShapeDtypeStruct(dims, jnp.float32)


def grids(rows, cols):
    return (
        lax.broadcasted_iota(jnp.int32, (rows, cols), 0),
        lax.broadcasted_iota(jnp.int32, (rows, cols), 1),
    )


def front_kernel(links, target, inverse, coupled, out, chosen, right, left, blocks, sems):
    rows = right.shape[0]
    moves = [
        pltpu.make_async_copy(source, place, sems.at[k])
        for k, (source, place) in enumerate(
            [(inverse, left), (target, right), (links, chosen), (coupled, blocks)]
        )
    ]
    for move in moves:
        move.start()
    moves[0].wait()
    moves[1].wait()
    out[:rows, :] = exact(left[...], right[...])
    moves[2].wait()
    moves[3].wait()
    matrix = jnp.zeros(left.shape, jnp.float32)
    for slot in range(blocks.shape[0]):
        matrix = matrix + jnp.where(chosen[slot] >= 0, blocks[slot], 0.0)
    out[rows:, :] = exact(left[...], matrix)


def packed(gram, half):
    i, j = grids(half, half)
    last = gram[half:, half:]
    corner = jnp.where(i >= j, gram[:half, :half], last)
    diagonal = jnp.sum(jnp.where(i == j, last, 0.0), axis=0, keepdims=True)
    return gram[half:, :half], corner, diagonal


def turned(count):
    line, odd = lax.axis_index("line"), 0
    for bit in range((count - 1).bit_length()):
        odd = odd ^ ((line >> bit) & 1)
    return odd


def gram_kernel(lines, scale, own, other, solved, piece):
    rows = own.shape[0] // 2
    half = own.shape[1] // 2
    section = lax.axis_index("sec")
    lead = section == 0
    first = jnp.where(lead, own[:rows, :], other[:rows, :])
    base = jnp.where(lead, other[:rows, :], own[:rows, :])
    carry = jnp.where(lead, other[rows:, :], own[rows:, :])
    second = base - exact(carry, first)
    solved[...] = jnp.where(lead, first, second)
    gram = (exact(first, first, TN) + exact(second, second, TN)) * scale
    block, corner, diagonal = packed(gram, half)
    piece[:half, :] = jnp.where(section == turned(lines), block, corner)
    piece[half:, :] = jnp.broadcast_to(diagonal, (piece.shape[0] - half, half))


def eliminate(gram, inverse, factor):
    size = gram.shape[0]
    i, j = grids(size, size)
    inverse[...] = jnp.where(i == j, 1.0, 0.0)
    factor[...] = jnp.zeros_like(factor)
    lane = lax.broadcasted_iota(jnp.int32, (1, size), 1)
    line = lax.broadcasted_iota(jnp.int32, (size, 1), 0)

    def step(k, carry):
        matrix = gram[...]
        pivot = jnp.sum(jnp.where((i == k) & (j == k), matrix, 0.0), axis=(0, 1), keepdims=True)
        root = lax.rsqrt(pivot)
        root = root * (1.5 - 0.5 * pivot * root * root)
        column = jnp.sum(jnp.where(j == k, matrix, 0.0), axis=1, keepdims=True) * root
        row = jnp.sum(jnp.where(i == k, matrix, 0.0), axis=0, keepdims=True) * root
        row = jnp.where(lane >= k, row, 0.0)
        column = jnp.where(line > k, column, 0.0)
        lead = jnp.sum(jnp.where(i == k, inverse[...], 0.0), axis=0, keepdims=True) * root
        gram[...] = matrix - column * row
        inverse[...] = jnp.where(i == k, lead, inverse[...] - column * lead)
        factor[...] = jnp.where(i == k, row, factor[...])
        return carry

    lax.fori_loop(0, size, step, 0)


def improved(error, weight, dot):
    lower = error * weight
    return weight * dot(lower, lower, NT) + (dot(lower, lower) - lower)


def factor_kernel(
    lines, mine, theirs, solved, panel, factor, gram_ref, inverse_ref, factor_ref
):
    half = mine.shape[1]
    size = 2 * half
    lead = lax.axis_index("sec") == turned(lines) if lines else True
    block = jnp.where(lead, mine[:half, :], theirs[:half, :])
    corner = jnp.where(lead, theirs[:half, :], mine[:half, :])
    diagonal = jnp.where(lead, theirs[half : half + 1, :], mine[half : half + 1, :])
    i, j = grids(half, half)
    mirrored = corner.T
    gram_ref[:half, :half] = jnp.where(i >= j, corner, mirrored)
    gram_ref[half:, half:] = jnp.where(i < j, corner, jnp.where(i == j, diagonal, mirrored))
    gram_ref[half:, :half] = block
    gram_ref[:half, half:] = block.T
    gram = gram_ref[...]

    i, j = grids(size, size)
    unit = jnp.where(i == j, 1.0, 0.0)
    weight = jnp.where(i > j, 1.0, jnp.where(i == j, 0.5, 0.0))
    spread = gram * unit
    row = lax.rsqrt(jnp.sum(spread, axis=0, keepdims=True))
    column = lax.rsqrt(jnp.sum(spread, axis=1, keepdims=True))
    scaled = gram * column * row
    step = improved(scaled - unit, weight, coarse)
    trial = unit + step
    product = coarse(trial, scaled)
    error = coarse(product, trial, NT) - unit
    trial = trial + coarse(improved(error, weight, coarse), trial)
    product = exact(trial, scaled)
    error = exact(product, trial, NT) - unit
    step = improved(error, weight, coarse)
    near = exact(solved[...] * row, trial, NT)
    panel[...] = near + middle(near, step, NT)
    upper = product + middle(step, product)
    factor[...] = jnp.where(i <= j, upper / row, 0.0)
    settled = jnp.max(jnp.abs(error)) < 0.02

    @pl.when(jnp.logical_not(settled))
    def _():
        eliminate(gram_ref, inverse_ref, factor_ref)
        panel[...] = exact(solved[...], inverse_ref[...], NT)
        factor[...] = factor_ref[...]


def finish(lines, mine, theirs, solved):
    rows, size = solved.shape
    scratch = [pltpu.VMEM((size, size), jnp.float32)] * 3
    return call(
        functools.partial(factor_kernel, lines),
        [shape(rows, size), shape(size, size)],
        [VMEM, VMEM, VMEM],
        "factor",
        24 * 2 * size**3,
        scratch,
    )(mine, theirs, solved)


def swap_lines(piece, lines):
    for bit in range((lines - 1).bit_length()):
        pairs = [(place, place ^ (2 << bit) ^ 1) for place in range(2 * lines)]
        piece = piece + lax.ppermute(piece, AXES, pairs)
    return piece


def two_sections(target, inverse, coupled, links, lines):
    rows, width = target.shape
    half = width // 2
    own = call(
        front_kernel,
        [shape(rows + inverse.shape[0], width)],
        [HBM, HBM, HBM, HBM],
        "front",
        4 * rows * rows * width,
        [
            pltpu.SMEM(links.shape, jnp.int32),
            pltpu.VMEM(target.shape, jnp.float32),
            pltpu.VMEM(inverse.shape, jnp.float32),
            pltpu.VMEM(coupled.shape, jnp.float32),
            pltpu.SemaphoreType.DMA((4,)),
        ],
    )(*(fetched(x) for x in (links, target, inverse, coupled)))[0]
    swap = [(0, 1), (1, 0)]
    other = lax.ppermute(own, "sec", swap)
    scale = 1.0 / (2 * lines * rows)
    solved, piece = call(
        functools.partial(gram_kernel, lines, scale),
        [shape(rows, width), shape(half + 8, half)],
        [VMEM, VMEM],
        "gram",
        6 * rows * rows * width,
    )(own, other)
    piece = swap_lines(piece, lines)
    theirs = lax.ppermute(piece, "sec", swap)
    return finish(lines, piece, theirs, solved)


def many_sections(target, inverse, coupled, links):
    section = lax.axis_index("sec")
    count = lax.axis_size("sec")
    acc = target
    solved = jnp.zeros_like(target)
    for anchor in range(count):
        mine = section == anchor
        candidate = jnp.where(mine, exact(inverse, acc), 0.0)
        arrived = lax.psum(candidate, "sec")
        solved = jnp.where(mine, arrived, solved)
        matrix = jnp.zeros_like(inverse)
        for slot in range(coupled.shape[0]):
            matrix = matrix + jnp.where(links[slot] == anchor, coupled[slot], 0.0)
        acc = acc - exact(matrix, arrived)
    total = lax.axis_size("line") * count * target.shape[0]
    gram = lax.psum(exact(solved, solved, TN), AXES) / total
    half = target.shape[1] // 2
    block, corner, diagonal = packed(gram, half)
    rest = jnp.broadcast_to(diagonal, (8, half))
    return finish(0, jnp.concatenate([block, rest]), jnp.concatenate([corner, rest]), solved)


def shards(right_side, inverse_diag, couplings, neighbors):
    local = (right_side[0, 0], inverse_diag[0, 0], couplings[0, 0], neighbors[0, 0])
    lines = lax.axis_size("line")
    if lax.axis_size("sec") == 2 and lines & (lines - 1) == 0:
        panel, factor = two_sections(*local, lines)
    else:
        panel, factor = many_sections(*local)
    return (panel[None, None], factor)


def solution(mesh):
    placed = (
        P("line", "sec", None, None),
        P("line", "sec", None, None),
        P("line", "sec", None, None, None),
        P("line", "sec", None),
    )
    return jax.shard_map(
        shards,
        mesh=mesh,
        in_specs=placed,
        out_specs=(P("line", "sec", None, None), P()),
        check_vma=False,
    )
```

```python
import functools

import jax
import jax.numpy as jnp
from jax import lax
from jax.experimental import pallas as pl
from jax.experimental.pallas import tpu as pltpu
from jax.sharding import PartitionSpec as P


AXES = ("line", "sec")
VMEM = pl.BlockSpec(memory_space=pltpu.VMEM)
HBM = pl.BlockSpec(memory_space=pltpu.HBM)
NN = (((1,), (0,)), ((), ()))
NT = (((1,), (1,)), ((), ()))
TN = (((0,), (0,)), ((), ()))


def terms(value, count=3):
    parts = []
    for _ in range(count):
        parts.append(value.astype(jnp.bfloat16))
        value = value - parts[-1].astype(jnp.float32)
    return parts


def product(left, right, dims=NN, order=2):
    total = None
    for level in range(order, -1, -1):
        for i in range(len(left)):
            if 0 <= level - i < len(right):
                part = lax.dot_general(
                    left[i], right[level - i], dims, preferred_element_type=jnp.float32
                )
                total = part if total is None else total + part
    return total


def exact(left, right, dims=NN):
    return product(terms(left), terms(right), dims)


def coarse(left, right, dims=NN):
    return product(terms(left, 1), terms(right, 1), dims)


def highest(left, right, dims=NN):
    return lax.dot_general(
        left, right, dims, precision=lax.Precision.HIGHEST, preferred_element_type=jnp.float32
    )


def call(kernel, outs, specs, name, flops, scratch=()):
    moved = sum(4 * out.size for out in outs)
    return pl.pallas_call(
        kernel,
        out_shape=outs,
        in_specs=specs,
        out_specs=[VMEM] * len(outs),
        scratch_shapes=list(scratch),
        compiler_params=pltpu.CompilerParams(vmem_limit_bytes=16 << 20),
        cost_estimate=pl.CostEstimate(flops=flops, bytes_accessed=moved, transcendentals=0),
        name=name,
    )


def fetched(value):
    return pltpu.with_memory_space_constraint(value, pltpu.HBM)


def shape(*dims):
    return jax.ShapeDtypeStruct(dims, jnp.float32)


def grids(rows, cols):
    return (
        lax.broadcasted_iota(jnp.int32, (rows, cols), 0),
        lax.broadcasted_iota(jnp.int32, (rows, cols), 1),
    )


def front_kernel(links, target, inverse, coupled, out, chosen, right, left, blocks, sems):
    rows = right.shape[0]
    moves = [
        pltpu.make_async_copy(source, place, sems.at[k])
        for k, (source, place) in enumerate(
            [(inverse, left), (target, right), (links, chosen), (coupled, blocks)]
        )
    ]
    for move in moves:
        move.start()
    moves[0].wait()
    moves[1].wait()
    lefts = terms(left[...])
    out[:rows, :] = product(lefts, terms(right[...]))
    moves[2].wait()
    moves[3].wait()
    matrix = jnp.zeros(left.shape, jnp.float32)
    for slot in range(blocks.shape[0]):
        matrix = matrix + jnp.where(chosen[slot] >= 0, blocks[slot], 0.0)
    out[rows:, :] = product(lefts, terms(matrix))


def packed(gram, half):
    i, j = grids(half, half)
    last = gram[half:, half:]
    corner = jnp.where(i >= j, gram[:half, :half], last)
    diagonal = jnp.sum(jnp.where(i == j, last, 0.0), axis=0, keepdims=True)
    return gram[half:, :half], corner, diagonal


def turned(count):
    line, odd = lax.axis_index("line"), 0
    for bit in range((count - 1).bit_length()):
        odd = odd ^ ((line >> bit) & 1)
    return odd


def gram_kernel(lines, scale, own, other, solved, piece):
    rows = own.shape[0] // 2
    half = own.shape[1] // 2
    section = lax.axis_index("sec")
    lead = section == 0
    first = jnp.where(lead, own[:rows, :], other[:rows, :])
    base = jnp.where(lead, other[:rows, :], own[:rows, :])
    carry = jnp.where(lead, other[rows:, :], own[rows:, :])
    firsts = terms(first)
    second = base - product(terms(carry), firsts)
    solved[...] = jnp.where(lead, first, second)
    seconds = terms(second)
    gram = (product(firsts, firsts, TN) + product(seconds, seconds, TN)) * scale
    block, corner, diagonal = packed(gram, half)
    piece[:half, :] = jnp.where(section == turned(lines), block, corner)
    piece[half:, :] = jnp.broadcast_to(diagonal, (piece.shape[0] - half, half))


def eliminate(gram, inverse, factor):
    size = gram.shape[0]
    i, j = grids(size, size)
    inverse[...] = jnp.where(i == j, 1.0, 0.0)
    factor[...] = jnp.zeros_like(factor)
    lane = lax.broadcasted_iota(jnp.int32, (1, size), 1)
    line = lax.broadcasted_iota(jnp.int32, (size, 1), 0)

    def step(k, carry):
        matrix = gram[...]
        pivot = jnp.sum(jnp.where((i == k) & (j == k), matrix, 0.0), axis=(0, 1), keepdims=True)
        root = lax.rsqrt(pivot)
        root = root * (1.5 - 0.5 * pivot * root * root)
        column = jnp.sum(jnp.where(j == k, matrix, 0.0), axis=1, keepdims=True) * root
        row = jnp.sum(jnp.where(i == k, matrix, 0.0), axis=0, keepdims=True) * root
        row = jnp.where(lane >= k, row, 0.0)
        column = jnp.where(line > k, column, 0.0)
        lead = jnp.sum(jnp.where(i == k, inverse[...], 0.0), axis=0, keepdims=True) * root
        gram[...] = matrix - column * row
        inverse[...] = jnp.where(i == k, lead, inverse[...] - column * lead)
        factor[...] = jnp.where(i == k, row, factor[...])
        return carry

    lax.fori_loop(0, size, step, 0)


def improved(error, weight):
    lower = error * weight
    rounded = terms(lower, 1)
    return weight * product(rounded, rounded, NT) + (product(rounded, rounded) - lower)


def factor_kernel(
    lines, mine, theirs, solved, panel, factor, gram_ref, inverse_ref, factor_ref
):
    half = mine.shape[1]
    size = 2 * half
    lead = lax.axis_index("sec") == turned(lines) if lines else True
    block = jnp.where(lead, mine[:half, :], theirs[:half, :])
    corner = jnp.where(lead, theirs[:half, :], mine[:half, :])
    diagonal = jnp.where(lead, theirs[half : half + 1, :], mine[half : half + 1, :])
    i, j = grids(half, half)
    mirrored = corner.T
    gram_ref[:half, :half] = jnp.where(i >= j, corner, mirrored)
    gram_ref[half:, half:] = jnp.where(i < j, corner, jnp.where(i == j, diagonal, mirrored))
    gram_ref[half:, :half] = block
    gram_ref[:half, half:] = block.T
    gram = gram_ref[...]

    i, j = grids(size, size)
    unit = jnp.where(i == j, 1.0, 0.0)
    weight = jnp.where(i > j, 1.0, jnp.where(i == j, 0.5, 0.0))
    spread = gram * unit
    row = lax.rsqrt(jnp.sum(spread, axis=0, keepdims=True))
    column = lax.rsqrt(jnp.sum(spread, axis=1, keepdims=True))
    scaled = gram * column * row
    scaleds = terms(scaled)
    step = improved(scaled - unit, weight)
    trial = unit + step
    error = coarse(product(terms(trial, 1), scaleds[:1]), trial, NT) - unit
    trial = terms(trial + coarse(improved(error, weight), trial), 1)
    upper = product(trial, scaleds)
    error = product(terms(upper), trial, NT) - unit
    step = terms(improved(error, weight), 2)
    near = product(terms(solved[...] * row), trial, NT)
    panel[...] = near + product(terms(near, 2), step, NT, 1)
    upper = upper + product(step, terms(upper, 2), NN, 1)
    factor[...] = jnp.where(i <= j, upper / row, 0.0)
    settled = jnp.max(jnp.abs(error)) < 0.02

    @pl.when(jnp.logical_not(settled))
    def _():
        eliminate(gram_ref, inverse_ref, factor_ref)
        panel[...] = exact(solved[...], inverse_ref[...], NT)
        factor[...] = factor_ref[...]


def finish(lines, mine, theirs, solved):
    rows, size = solved.shape
    scratch = [pltpu.VMEM((size, size), jnp.float32)] * 3
    return call(
        functools.partial(factor_kernel, lines),
        [shape(rows, size), shape(size, size)],
        [VMEM, VMEM, VMEM],
        "factor",
        24 * 2 * size**3,
        scratch,
    )(mine, theirs, solved)


def swap_lines(piece, lines):
    bits = (lines - 1).bit_length()
    low, high = range(bits // 2), range(bits // 2, bits)
    orders = [[], []]
    for k in range(bits - bits // 2):
        pair = [group[k] for group in (low, high) if k < len(group)]
        orders[0] += pair
        orders[1] += pair[::-1]
    for step in range(bits):
        pairs = []
        for place in range(2 * lines):
            bit = orders[place & 1 ^ (place >> 1).bit_count() & 1][step]
            pairs.append((place, place ^ (2 << bit) ^ 1))
        piece = piece + lax.ppermute(piece, AXES, pairs)
    return piece


def two_sections(target, inverse, coupled, links, lines):
    rows, width = target.shape
    half = width // 2
    own = call(
        front_kernel,
        [shape(rows + inverse.shape[0], width)],
        [HBM, HBM, HBM, HBM],
        "front",
        4 * rows * rows * width,
        [
            pltpu.SMEM(links.shape, jnp.int32),
            pltpu.VMEM(target.shape, jnp.float32),
            pltpu.VMEM(inverse.shape, jnp.float32),
            pltpu.VMEM(coupled.shape, jnp.float32),
            pltpu.SemaphoreType.DMA((4,)),
        ],
    )(*(fetched(x) for x in (links, target, inverse, coupled)))[0]
    swap = [(0, 1), (1, 0)]
    other = lax.ppermute(own, "sec", swap)
    scale = 1.0 / (2 * lines * rows)
    solved, piece = call(
        functools.partial(gram_kernel, lines, scale),
        [shape(rows, width), shape(half + 8, half)],
        [VMEM, VMEM],
        "gram",
        6 * rows * rows * width,
    )(own, other)
    piece = swap_lines(piece, lines)
    theirs = lax.ppermute(piece, "sec", swap)
    return finish(lines, piece, theirs, solved)


def many_sections(target, inverse, coupled, links):
    section = lax.axis_index("sec")
    count = lax.axis_size("sec")
    acc = target
    solved = jnp.zeros_like(target)
    for anchor in range(count):
        mine = section == anchor
        candidate = jnp.where(mine, highest(inverse, acc), 0.0)
        arrived = lax.psum(candidate, "sec")
        solved = jnp.where(mine, arrived, solved)
        matrix = jnp.zeros_like(inverse)
        for slot in range(coupled.shape[0]):
            matrix = matrix + jnp.where(links[slot] == anchor, coupled[slot], 0.0)
        acc = acc - highest(matrix, arrived)
    total = lax.axis_size("line") * count * target.shape[0]
    gram = lax.psum(highest(solved, solved, TN), AXES) / total
    half = target.shape[1] // 2
    block, corner, diagonal = packed(gram, half)
    rest = jnp.broadcast_to(diagonal, (8, half))
    return finish(0, jnp.concatenate([block, rest]), jnp.concatenate([corner, rest]), solved)


def shards(right_side, inverse_diag, couplings, neighbors):
    local = (right_side[0, 0], inverse_diag[0, 0], couplings[0, 0], neighbors[0, 0])
    lines = lax.axis_size("line")
    if lax.axis_size("sec") == 2 and lines & (lines - 1) == 0:
        panel, factor = two_sections(*local, lines)
    else:
        panel, factor = many_sections(*local)
    return (panel[None, None], factor)


def solution(mesh):
    placed = (
        P("line", "sec", None, None),
        P("line", "sec", None, None),
        P("line", "sec", None, None, None),
        P("line", "sec", None),
    )
    return jax.shard_map(
        shards,
        mesh=mesh,
        in_specs=placed,
        out_specs=(P("line", "sec", None, None), P()),
        check_vma=False,
    )
```

```python
import functools

import jax
import jax.numpy as jnp
from jax import lax
from jax.experimental import pallas as pl
from jax.experimental.pallas import tpu as pltpu
from jax.sharding import PartitionSpec as P


AXES = ("line", "sec")
VMEM = pl.BlockSpec(memory_space=pltpu.VMEM)
HBM = pl.BlockSpec(memory_space=pltpu.HBM)
NN = (((1,), (0,)), ((), ()))
NT = (((1,), (1,)), ((), ()))
TN = (((0,), (0,)), ((), ()))


def terms(value, count=3):
    parts = []
    for _ in range(count):
        parts.append(value.astype(jnp.bfloat16))
        value = value - parts[-1].astype(jnp.float32)
    return parts


def product(left, right, dims=NN, order=2):
    total = None
    for level in range(order, -1, -1):
        for i in range(len(left)):
            if 0 <= level - i < len(right):
                part = lax.dot_general(
                    left[i], right[level - i], dims, preferred_element_type=jnp.float32
                )
                total = part if total is None else total + part
    return total


def exact(left, right, dims=NN):
    return product(terms(left), terms(right), dims)


def coarse(left, right, dims=NN):
    return product(terms(left, 1), terms(right, 1), dims)


def highest(left, right, dims=NN):
    return lax.dot_general(
        left, right, dims, precision=lax.Precision.HIGHEST, preferred_element_type=jnp.float32
    )


def call(kernel, outs, specs, name, flops, scratch=(), place=VMEM):
    moved = sum(4 * out.size for out in outs)
    return pl.pallas_call(
        kernel,
        out_shape=outs,
        in_specs=specs,
        out_specs=[place] * len(outs),
        scratch_shapes=list(scratch),
        compiler_params=pltpu.CompilerParams(vmem_limit_bytes=16 << 20),
        cost_estimate=pl.CostEstimate(flops=flops, bytes_accessed=moved, transcendentals=0),
        name=name,
    )


def fetched(value):
    return pltpu.with_memory_space_constraint(value, pltpu.HBM)


def shape(*dims):
    return jax.ShapeDtypeStruct(dims, jnp.float32)


def grids(rows, cols):
    return (
        lax.broadcasted_iota(jnp.int32, (rows, cols), 0),
        lax.broadcasted_iota(jnp.int32, (rows, cols), 1),
    )


def front_kernel(links, target, inverse, coupled, out, chosen, right, left, blocks, sems):
    rows = right.shape[0]
    moves = [
        pltpu.make_async_copy(source, place, sems.at[k])
        for k, (source, place) in enumerate(
            [(inverse, left), (target, right), (links, chosen), (coupled, blocks)]
        )
    ]
    for move in moves:
        move.start()
    moves[0].wait()
    moves[1].wait()
    lefts = terms(left[...])
    out[:rows, :] = product(lefts, terms(right[...]))
    moves[2].wait()
    moves[3].wait()
    matrix = jnp.zeros(left.shape, jnp.float32)
    for slot in range(blocks.shape[0]):
        matrix = matrix + jnp.where(chosen[slot] >= 0, blocks[slot], 0.0)
    out[rows:, :] = product(lefts, terms(matrix))


def packed(gram, half):
    i, j = grids(half, half)
    last = gram[half:, half:]
    corner = jnp.where(i >= j, gram[:half, :half], last)
    diagonal = jnp.sum(jnp.where(i == j, last, 0.0), axis=0, keepdims=True)
    return gram[half:, :half], corner, diagonal


def turned(count):
    line, odd = lax.axis_index("line"), 0
    for bit in range((count - 1).bit_length()):
        odd = odd ^ ((line >> bit) & 1)
    return odd


def gram_kernel(lines, scale, own, other, solved, piece):
    rows = own.shape[0] // 2
    half = own.shape[1] // 2
    section = lax.axis_index("sec")
    lead = section == 0
    first = jnp.where(lead, own[:rows, :], other[:rows, :])
    base = jnp.where(lead, other[:rows, :], own[:rows, :])
    carry = jnp.where(lead, other[rows:, :], own[rows:, :])
    firsts = terms(first)
    second = base - product(terms(carry), firsts)
    solved[...] = jnp.where(lead, first, second)
    seconds = terms(second)
    gram = (product(firsts, firsts, TN) + product(seconds, seconds, TN)) * scale
    block, corner, diagonal = packed(gram, half)
    piece[:half, :] = jnp.where(section == turned(lines), block, corner)
    piece[half:, :] = jnp.broadcast_to(diagonal, (piece.shape[0] - half, half))


def eliminate(gram, inverse, factor):
    size = gram.shape[0]
    i, j = grids(size, size)
    inverse[...] = jnp.where(i == j, 1.0, 0.0)
    factor[...] = jnp.zeros_like(factor)
    lane = lax.broadcasted_iota(jnp.int32, (1, size), 1)
    line = lax.broadcasted_iota(jnp.int32, (size, 1), 0)

    def step(k, carry):
        matrix = gram[...]
        pivot = jnp.sum(jnp.where((i == k) & (j == k), matrix, 0.0), axis=(0, 1), keepdims=True)
        root = lax.rsqrt(pivot)
        root = root * (1.5 - 0.5 * pivot * root * root)
        column = jnp.sum(jnp.where(j == k, matrix, 0.0), axis=1, keepdims=True) * root
        row = jnp.sum(jnp.where(i == k, matrix, 0.0), axis=0, keepdims=True) * root
        row = jnp.where(lane >= k, row, 0.0)
        column = jnp.where(line > k, column, 0.0)
        lead = jnp.sum(jnp.where(i == k, inverse[...], 0.0), axis=0, keepdims=True) * root
        gram[...] = matrix - column * row
        inverse[...] = jnp.where(i == k, lead, inverse[...] - column * lead)
        factor[...] = jnp.where(i == k, row, factor[...])
        return carry

    lax.fori_loop(0, size, step, 0)


def improved(error, weight):
    lower = error * weight
    rounded = terms(lower, 1)
    return weight * product(rounded, rounded, NT) + (product(rounded, rounded) - lower)


def factor_kernel(lines, mine, theirs, solved, panel, factor, gram_ref, inverse_ref, factor_ref, panel_ref, sems):
    half = mine.shape[1]
    size = 2 * half
    lead = lax.axis_index("sec") == turned(lines) if lines else True
    block = jnp.where(lead, mine[:half, :], theirs[:half, :])
    corner = jnp.where(lead, theirs[:half, :], mine[:half, :])
    diagonal = jnp.where(lead, theirs[half : half + 1, :], mine[half : half + 1, :])
    i, j = grids(half, half)
    mirrored = corner.T
    gram_ref[:half, :half] = jnp.where(i >= j, corner, mirrored)
    gram_ref[half:, half:] = jnp.where(i < j, corner, jnp.where(i == j, diagonal, mirrored))
    gram_ref[half:, :half] = block
    gram_ref[:half, half:] = block.T
    gram = gram_ref[...]

    i, j = grids(size, size)
    unit = jnp.where(i == j, 1.0, 0.0)
    weight = jnp.where(i > j, 1.0, jnp.where(i == j, 0.5, 0.0))
    spread = gram * unit
    row = lax.rsqrt(jnp.sum(spread, axis=0, keepdims=True))
    column = lax.rsqrt(jnp.sum(spread, axis=1, keepdims=True))
    scaled = gram * column * row
    scaleds = terms(scaled)
    trial = unit - (scaled - unit) * weight
    error = coarse(product(terms(trial, 1), scaleds[:1]), trial, NT) - unit
    trial = terms(trial + coarse(improved(error, weight), trial), 1)
    upper = product(trial, scaleds)
    error = product(terms(upper), trial, NT) - unit
    step = terms(improved(error, weight), 2)
    upper = upper + product(step, terms(upper, 2), NN, 1)
    factor_ref[...] = jnp.where(i <= j, upper / row, 0.0)
    moves = [
        pltpu.make_async_copy(source, place, sems.at[k])
        for k, (source, place) in enumerate([(factor_ref, factor), (panel_ref, panel)])
    ]
    moves[0].start()
    near = product(terms(solved[...] * row), trial, NT)
    panel_ref[...] = near + product(terms(near, 2), step, NT, 1)
    moves[1].start()
    last = trial[0].astype(jnp.float32) + product(step, trial)
    error = product(terms(upper), terms(last), NT) - unit
    settled = jnp.max(jnp.abs(error)) < 1e-5
    moves[0].wait()
    moves[1].wait()

    @pl.when(jnp.logical_not(settled))
    def _():
        eliminate(gram_ref, inverse_ref, factor_ref)
        panel_ref[...] = exact(solved[...], inverse_ref[...], NT)
        for move in moves:
            move.start()
        for move in moves:
            move.wait()


def finish(lines, mine, theirs, solved):
    rows, size = solved.shape
    scratch = [pltpu.VMEM((size, size), jnp.float32)] * 3
    scratch += [pltpu.VMEM((rows, size), jnp.float32), pltpu.SemaphoreType.DMA((2,))]
    return call(
        functools.partial(factor_kernel, lines),
        [shape(rows, size), shape(size, size)],
        [VMEM, VMEM, VMEM],
        "factor",
        24 * 2 * size**3,
        scratch,
        HBM,
    )(mine, theirs, solved)


def paired(lines, masks):
    pairs = []
    for place in range(2 * lines):
        mask = masks[place & 1 ^ (place >> 1).bit_count() & 1]
        pairs.append((place, place ^ 2 * mask ^ mask.bit_count() & 1))
    return pairs


def swap_lines(piece, lines):
    bits = (lines - 1).bit_length()
    groups = [[1 << b, 2 << b, 3 << b] for b in range(0, bits - 1, 2)]
    turn = len(groups) // 2
    for one, two in zip(groups, groups[turn:] + groups[:turn]):
        a, b, c = (lax.ppermute(piece, AXES, paired(lines, masks)) for masks in zip(one, two))
        piece = (piece + a) + (b + c)
    if bits % 2:
        mask = 1 << bits - 1
        piece = piece + lax.ppermute(piece, AXES, paired(lines, (mask, mask)))
    return piece


def two_sections(target, inverse, coupled, links, lines):
    rows, width = target.shape
    half = width // 2
    own = call(
        front_kernel,
        [shape(rows + inverse.shape[0], width)],
        [HBM, HBM, HBM, HBM],
        "front",
        4 * rows * rows * width,
        [
            pltpu.SMEM(links.shape, jnp.int32),
            pltpu.VMEM(target.shape, jnp.float32),
            pltpu.VMEM(inverse.shape, jnp.float32),
            pltpu.VMEM(coupled.shape, jnp.float32),
            pltpu.SemaphoreType.DMA((4,)),
        ],
    )(*(fetched(x) for x in (links, target, inverse, coupled)))[0]
    swap = [(0, 1), (1, 0)]
    other = lax.ppermute(own, "sec", swap)
    scale = 1.0 / (2 * lines * rows)
    solved, piece = call(
        functools.partial(gram_kernel, lines, scale),
        [shape(rows, width), shape(half + 8, half)],
        [VMEM, VMEM],
        "gram",
        6 * rows * rows * width,
    )(own, other)
    piece = swap_lines(piece, lines)
    theirs = lax.ppermute(piece, "sec", swap)
    return finish(lines, piece, theirs, solved)


def many_sections(target, inverse, coupled, links):
    section = lax.axis_index("sec")
    count = lax.axis_size("sec")
    acc = target
    solved = jnp.zeros_like(target)
    for anchor in range(count):
        mine = section == anchor
        candidate = jnp.where(mine, highest(inverse, acc), 0.0)
        arrived = lax.psum(candidate, "sec")
        solved = jnp.where(mine, arrived, solved)
        matrix = jnp.zeros_like(inverse)
        for slot in range(coupled.shape[0]):
            matrix = matrix + jnp.where(links[slot] == anchor, coupled[slot], 0.0)
        acc = acc - highest(matrix, arrived)
    total = lax.axis_size("line") * count * target.shape[0]
    gram = lax.psum(highest(solved, solved, TN), AXES) / total
    half = target.shape[1] // 2
    block, corner, diagonal = packed(gram, half)
    rest = jnp.broadcast_to(diagonal, (8, half))
    return finish(0, jnp.concatenate([block, rest]), jnp.concatenate([corner, rest]), solved)


def shards(right_side, inverse_diag, couplings, neighbors):
    local = (right_side[0, 0], inverse_diag[0, 0], couplings[0, 0], neighbors[0, 0])
    lines = lax.axis_size("line")
    if lax.axis_size("sec") == 2 and lines & (lines - 1) == 0:
        panel, factor = two_sections(*local, lines)
    else:
        panel, factor = many_sections(*local)
    return (panel[None, None], factor)


def solution(mesh):
    placed = (
        P("line", "sec", None, None),
        P("line", "sec", None, None),
        P("line", "sec", None, None, None),
        P("line", "sec", None),
    )
    return jax.shard_map(
        shards,
        mesh=mesh,
        in_specs=placed,
        out_specs=(P("line", "sec", None, None), P()),
        check_vma=False,
    )
```

```python
import functools

import jax
import jax.numpy as jnp
from jax import lax
from jax.experimental import pallas as pl
from jax.experimental.pallas import tpu as pltpu
from jax.sharding import PartitionSpec as P


AXES = ("line", "sec")
VMEM = pl.BlockSpec(memory_space=pltpu.VMEM)
HBM = pl.BlockSpec(memory_space=pltpu.HBM)
NN = (((1,), (0,)), ((), ()))
NT = (((1,), (1,)), ((), ()))
TN = (((0,), (0,)), ((), ()))


def terms(value, count=3):
    parts = []
    for _ in range(count):
        parts.append(value.astype(jnp.bfloat16))
        value = value - parts[-1].astype(jnp.float32)
    return parts


def product(left, right, dims=NN, order=2):
    total = None
    for level in range(order, -1, -1):
        for i in range(len(left)):
            if 0 <= level - i < len(right):
                part = lax.dot_general(
                    left[i], right[level - i], dims, preferred_element_type=jnp.float32
                )
                total = part if total is None else total + part
    return total


def exact(left, right, dims=NN):
    return product(terms(left), terms(right), dims)


def coarse(left, right, dims=NN):
    return product(terms(left, 1), terms(right, 1), dims)


def highest(left, right, dims=NN):
    return lax.dot_general(
        left, right, dims, precision=lax.Precision.HIGHEST, preferred_element_type=jnp.float32
    )


def call(kernel, outs, specs, name, flops, scratch=(), place=VMEM):
    moved = sum(4 * out.size for out in outs)
    return pl.pallas_call(
        kernel,
        out_shape=outs,
        in_specs=specs,
        out_specs=[place] * len(outs),
        scratch_shapes=list(scratch),
        compiler_params=pltpu.CompilerParams(vmem_limit_bytes=16 << 20),
        cost_estimate=pl.CostEstimate(flops=flops, bytes_accessed=moved, transcendentals=0),
        name=name,
    )


def fetched(value):
    return pltpu.with_memory_space_constraint(value, pltpu.HBM)


def shape(*dims):
    return jax.ShapeDtypeStruct(dims, jnp.float32)


def grids(rows, cols):
    return (
        lax.broadcasted_iota(jnp.int32, (rows, cols), 0),
        lax.broadcasted_iota(jnp.int32, (rows, cols), 1),
    )


def front_kernel(links, target, inverse, coupled, out, chosen, right, left, blocks, sems):
    rows = right.shape[0]
    moves = [
        pltpu.make_async_copy(source, place, sems.at[k])
        for k, (source, place) in enumerate(
            [(inverse, left), (target, right), (links, chosen), (coupled, blocks)]
        )
    ]
    for move in moves:
        move.start()
    moves[0].wait()
    moves[1].wait()
    lefts = terms(left[...], 2)
    out[:rows, :] = product(lefts, terms(right[...], 2), NN, 1)
    moves[2].wait()
    moves[3].wait()
    matrix = jnp.zeros(left.shape, jnp.float32)
    for slot in range(blocks.shape[0]):
        matrix = matrix + jnp.where(chosen[slot] >= 0, blocks[slot], 0.0)
    out[rows:, :] = product(lefts, terms(matrix, 2), NN, 1)


def packed(gram, half):
    i, j = grids(half, half)
    last = gram[half:, half:]
    corner = jnp.where(i >= j, gram[:half, :half], last)
    diagonal = jnp.sum(jnp.where(i == j, last, 0.0), axis=0, keepdims=True)
    return gram[half:, :half], corner, diagonal


def turned(count):
    line, odd = lax.axis_index("line"), 0
    for bit in range((count - 1).bit_length()):
        odd = odd ^ ((line >> bit) & 1)
    return odd


def gram_kernel(lines, scale, own, other, solved, piece):
    rows = own.shape[0] // 2
    half = own.shape[1] // 2
    section = lax.axis_index("sec")
    lead = section == 0
    first = jnp.where(lead, own[:rows, :], other[:rows, :])
    base = jnp.where(lead, other[:rows, :], own[:rows, :])
    carry = jnp.where(lead, other[rows:, :], own[rows:, :])
    firsts = terms(first, 2)
    second = base - product(terms(carry, 2), firsts, NN, 1)
    solved[...] = jnp.where(lead, first, second)
    seconds = terms(second, 2)
    gram = (product(firsts, firsts, TN) + product(seconds, seconds, TN)) * scale
    block, corner, diagonal = packed(gram, half)
    piece[:half, :] = jnp.where(section == turned(lines), block, corner)
    piece[half:, :] = jnp.broadcast_to(diagonal, (piece.shape[0] - half, half))


def eliminate(gram, inverse, factor):
    size = gram.shape[0]
    i, j = grids(size, size)
    inverse[...] = jnp.where(i == j, 1.0, 0.0)
    factor[...] = jnp.zeros_like(factor)
    lane = lax.broadcasted_iota(jnp.int32, (1, size), 1)
    line = lax.broadcasted_iota(jnp.int32, (size, 1), 0)

    def step(k, carry):
        matrix = gram[...]
        pivot = jnp.sum(jnp.where((i == k) & (j == k), matrix, 0.0), axis=(0, 1), keepdims=True)
        root = lax.rsqrt(pivot)
        root = root * (1.5 - 0.5 * pivot * root * root)
        column = jnp.sum(jnp.where(j == k, matrix, 0.0), axis=1, keepdims=True) * root
        row = jnp.sum(jnp.where(i == k, matrix, 0.0), axis=0, keepdims=True) * root
        row = jnp.where(lane >= k, row, 0.0)
        column = jnp.where(line > k, column, 0.0)
        lead = jnp.sum(jnp.where(i == k, inverse[...], 0.0), axis=0, keepdims=True) * root
        gram[...] = matrix - column * row
        inverse[...] = jnp.where(i == k, lead, inverse[...] - column * lead)
        factor[...] = jnp.where(i == k, row, factor[...])
        return carry

    lax.fori_loop(0, size, step, 0)


def improved(error, weight):
    lower = error * weight
    rounded = terms(lower, 1)
    return weight * product(rounded, rounded, NT) + (product(rounded, rounded) - lower)


def factor_kernel(lines, mine, theirs, solved, panel, factor, gram_ref, inverse_ref, factor_ref, panel_ref, sems):
    half = mine.shape[1]
    size = 2 * half
    lead = lax.axis_index("sec") == turned(lines) if lines else True
    block = jnp.where(lead, mine[:half, :], theirs[:half, :])
    corner = jnp.where(lead, theirs[:half, :], mine[:half, :])
    diagonal = jnp.where(lead, theirs[half : half + 1, :], mine[half : half + 1, :])
    i, j = grids(half, half)
    mirrored = corner.T
    gram_ref[:half, :half] = jnp.where(i >= j, corner, mirrored)
    gram_ref[half:, half:] = jnp.where(i < j, corner, jnp.where(i == j, diagonal, mirrored))
    gram_ref[half:, :half] = block
    gram_ref[:half, half:] = block.T
    gram = gram_ref[...]

    i, j = grids(size, size)
    unit = jnp.where(i == j, 1.0, 0.0)
    weight = jnp.where(i > j, 1.0, jnp.where(i == j, 0.5, 0.0))
    spread = gram * unit
    row = lax.rsqrt(jnp.sum(spread, axis=0, keepdims=True))
    column = lax.rsqrt(jnp.sum(spread, axis=1, keepdims=True))
    scaled = gram * column * row
    scaleds = terms(scaled)
    solveds = terms(solved[...] * row)
    moves = [
        pltpu.make_async_copy(source, place, sems.at[k])
        for k, (source, place) in enumerate([(panel_ref, panel), (factor_ref, factor)])
    ]

    def attempt(trial):
        upper = product(trial, scaleds)
        near = product(solveds, trial, NT)
        error = product(terms(upper), trial, NT) - unit
        step = terms(improved(error, weight), 2)
        panel_ref[...] = near + product(terms(near, 2), step, NT, 1)
        moves[0].start()
        upper = upper + product(step, terms(upper, 2), NN, 1)
        factor_ref[...] = jnp.where(i <= j, upper / row, 0.0)
        moves[1].start()
        last = trial[0].astype(jnp.float32) + product(step, trial)
        error = product(terms(upper, 2), terms(last, 2), NT, 1) - unit
        open_entries = jnp.sum(jnp.where(jnp.abs(error) < 3e-5, 0.0, 1.0))
        moves[0].wait()
        moves[1].wait()
        return last, open_entries > 0.0

    trial = unit - (scaled - unit) * weight
    error = coarse(product(terms(trial, 1), scaleds[:1]), trial, NT) - unit
    trial = trial + coarse(improved(error, weight), trial)
    trial, unsettled = attempt(terms(trial, 1))

    @pl.when(unsettled)
    def _():
        _, again = attempt(terms(trial, 1))

        @pl.when(again)
        def _():
            eliminate(gram_ref, inverse_ref, factor_ref)
            panel_ref[...] = exact(solved[...], inverse_ref[...], NT)
            for move in moves:
                move.start()
            for move in moves:
                move.wait()


def finish(lines, mine, theirs, solved):
    rows, size = solved.shape
    scratch = [pltpu.VMEM((size, size), jnp.float32)] * 3
    scratch += [pltpu.VMEM((rows, size), jnp.float32), pltpu.SemaphoreType.DMA((2,))]
    return call(
        functools.partial(factor_kernel, lines),
        [shape(rows, size), shape(size, size)],
        [VMEM, VMEM, VMEM],
        "factor",
        24 * 2 * size**3,
        scratch,
        HBM,
    )(mine, theirs, solved)


def paired(lines, masks):
    pairs = []
    for place in range(2 * lines):
        mask = masks[place & 1 ^ (place >> 1).bit_count() & 1]
        pairs.append((place, place ^ 2 * mask ^ mask.bit_count() & 1))
    return pairs


def swap_lines(piece, lines):
    bits = (lines - 1).bit_length()
    groups = [[1 << b, 2 << b, 3 << b] for b in range(0, bits - 1, 2)]
    turn = len(groups) // 2
    for one, two in zip(groups, groups[turn:] + groups[:turn]):
        a, b, c = (lax.ppermute(piece, AXES, paired(lines, masks)) for masks in zip(one, two))
        piece = (piece + a) + (b + c)
    if bits % 2:
        mask = 1 << bits - 1
        piece = piece + lax.ppermute(piece, AXES, paired(lines, (mask, mask)))
    return piece


def two_sections(target, inverse, coupled, links, lines):
    rows, width = target.shape
    half = width // 2
    own = call(
        front_kernel,
        [shape(rows + inverse.shape[0], width)],
        [HBM, HBM, HBM, HBM],
        "front",
        4 * rows * rows * width,
        [
            pltpu.SMEM(links.shape, jnp.int32),
            pltpu.VMEM(target.shape, jnp.float32),
            pltpu.VMEM(inverse.shape, jnp.float32),
            pltpu.VMEM(coupled.shape, jnp.float32),
            pltpu.SemaphoreType.DMA((4,)),
        ],
    )(*(fetched(x) for x in (links, target, inverse, coupled)))[0]
    swap = [(0, 1), (1, 0)]
    other = lax.ppermute(own, "sec", swap)
    scale = 1.0 / (2 * lines * rows)
    solved, piece = call(
        functools.partial(gram_kernel, lines, scale),
        [shape(rows, width), shape(half + 8, half)],
        [VMEM, VMEM],
        "gram",
        6 * rows * rows * width,
    )(own, other)
    piece = swap_lines(piece, lines)
    theirs = lax.ppermute(piece, "sec", swap)
    return finish(lines, piece, theirs, solved)


def many_sections(target, inverse, coupled, links):
    section = lax.axis_index("sec")
    count = lax.axis_size("sec")
    acc = target
    solved = jnp.zeros_like(target)
    for anchor in range(count):
        mine = section == anchor
        candidate = jnp.where(mine, highest(inverse, acc), 0.0)
        arrived = lax.psum(candidate, "sec")
        solved = jnp.where(mine, arrived, solved)
        matrix = jnp.zeros_like(inverse)
        for slot in range(coupled.shape[0]):
            matrix = matrix + jnp.where(links[slot] == anchor, coupled[slot], 0.0)
        acc = acc - highest(matrix, arrived)
    total = lax.axis_size("line") * count * target.shape[0]
    gram = lax.psum(highest(solved, solved, TN), AXES) / total
    half = target.shape[1] // 2
    block, corner, diagonal = packed(gram, half)
    rest = jnp.broadcast_to(diagonal, (8, half))
    return finish(0, jnp.concatenate([block, rest]), jnp.concatenate([corner, rest]), solved)


def shards(right_side, inverse_diag, couplings, neighbors):
    local = (right_side[0, 0], inverse_diag[0, 0], couplings[0, 0], neighbors[0, 0])
    lines = lax.axis_size("line")
    if lax.axis_size("sec") == 2 and lines & (lines - 1) == 0:
        panel, factor = two_sections(*local, lines)
    else:
        panel, factor = many_sections(*local)
    return (panel[None, None], factor)


def solution(mesh):
    placed = (
        P("line", "sec", None, None),
        P("line", "sec", None, None),
        P("line", "sec", None, None, None),
        P("line", "sec", None),
    )
    return jax.shard_map(
        shards,
        mesh=mesh,
        in_specs=placed,
        out_specs=(P("line", "sec", None, None), P()),
        check_vma=False,
    )
```

```python
import functools

import jax
import jax.numpy as jnp
from jax import lax
from jax.experimental import pallas as pl
from jax.experimental.pallas import tpu as pltpu
from jax.sharding import PartitionSpec as P


AXES = ("line", "sec")
VMEM = pl.BlockSpec(memory_space=pltpu.VMEM)
HBM = pl.BlockSpec(memory_space=pltpu.HBM)
NN = (((1,), (0,)), ((), ()))
NT = (((1,), (1,)), ((), ()))
TN = (((0,), (0,)), ((), ()))


def terms(value, count=3):
    parts = []
    for _ in range(count):
        parts.append(value.astype(jnp.bfloat16))
        value = value - parts[-1].astype(jnp.float32)
    return parts


def product(left, right, dims=NN, order=2):
    total = None
    for level in range(order, -1, -1):
        for i in range(len(left)):
            if 0 <= level - i < len(right):
                part = lax.dot_general(
                    left[i], right[level - i], dims, preferred_element_type=jnp.float32
                )
                total = part if total is None else total + part
    return total


def exact(left, right, dims=NN):
    return product(terms(left), terms(right), dims)


def coarse(left, right, dims=NN):
    return product(terms(left, 1), terms(right, 1), dims)


def highest(left, right, dims=NN):
    return lax.dot_general(
        left, right, dims, precision=lax.Precision.HIGHEST, preferred_element_type=jnp.float32
    )


def call(kernel, outs, specs, name, flops, scratch=(), place=VMEM):
    moved = sum(4 * out.size for out in outs)
    return pl.pallas_call(
        kernel,
        out_shape=outs,
        in_specs=specs,
        out_specs=[place] * len(outs),
        scratch_shapes=list(scratch),
        compiler_params=pltpu.CompilerParams(vmem_limit_bytes=16 << 20),
        cost_estimate=pl.CostEstimate(flops=flops, bytes_accessed=moved, transcendentals=0),
        name=name,
    )


def fetched(value):
    return pltpu.with_memory_space_constraint(value, pltpu.HBM)


def shape(*dims):
    return jax.ShapeDtypeStruct(dims, jnp.float32)


def grids(rows, cols):
    return (
        lax.broadcasted_iota(jnp.int32, (rows, cols), 0),
        lax.broadcasted_iota(jnp.int32, (rows, cols), 1),
    )


def front_kernel(links, target, inverse, coupled, out, chosen, right, left, blocks, sems):
    rows = right.shape[0]
    moves = [
        pltpu.make_async_copy(source, place, sems.at[k])
        for k, (source, place) in enumerate(
            [(inverse, left), (target, right), (links, chosen), (coupled, blocks)]
        )
    ]
    for move in moves:
        move.start()
    moves[0].wait()
    moves[1].wait()
    lefts = terms(left[...], 2)
    out[:rows, :] = product(lefts, terms(right[...], 2), NN, 1)
    moves[2].wait()
    moves[3].wait()
    matrix = jnp.zeros(left.shape, jnp.float32)
    for slot in range(blocks.shape[0]):
        matrix = matrix + jnp.where(chosen[slot] >= 0, blocks[slot], 0.0)
    out[rows:, :] = product(lefts, terms(matrix, 2), NN, 1)


def packed(gram, half):
    i, j = grids(half, half)
    last = gram[half:, half:]
    corner = jnp.where(i >= j, gram[:half, :half], last)
    diagonal = jnp.sum(jnp.where(i == j, last, 0.0), axis=0, keepdims=True)
    return gram[half:, :half], corner, diagonal


def turned(count):
    line = lax.axis_index("line")
    return sum((line >> bit) & 1 for bit in turning(count)) % 2


def turning(count):
    return sorted({0, max((count - 1).bit_length() - 1, 0)})


def gram_kernel(lines, scale, own, other, solved, piece):
    rows = own.shape[0] // 2
    half = own.shape[1] // 2
    section = lax.axis_index("sec")
    lead = section == 0
    first = jnp.where(lead, own[:rows, :], other[:rows, :])
    base = jnp.where(lead, other[:rows, :], own[:rows, :])
    carry = jnp.where(lead, other[rows:, :], own[rows:, :])
    firsts = terms(first, 2)
    second = base - product(terms(carry, 2), firsts, NN, 1)
    solved[...] = jnp.where(lead, first, second)
    seconds = terms(second, 2)
    gram = (product(firsts, firsts, TN) + product(seconds, seconds, TN)) * scale
    block, corner, diagonal = packed(gram, half)
    piece[:half, :] = jnp.where(section == turned(lines), block, corner)
    piece[half:, :] = jnp.broadcast_to(diagonal, (piece.shape[0] - half, half))


def eliminate(gram, inverse, factor):
    size = gram.shape[0]
    i, j = grids(size, size)
    inverse[...] = jnp.where(i == j, 1.0, 0.0)
    factor[...] = jnp.zeros_like(factor)
    lane = lax.broadcasted_iota(jnp.int32, (1, size), 1)
    line = lax.broadcasted_iota(jnp.int32, (size, 1), 0)

    def step(k, carry):
        matrix = gram[...]
        pivot = jnp.sum(jnp.where((i == k) & (j == k), matrix, 0.0), axis=(0, 1), keepdims=True)
        root = lax.rsqrt(pivot)
        root = root * (1.5 - 0.5 * pivot * root * root)
        column = jnp.sum(jnp.where(j == k, matrix, 0.0), axis=1, keepdims=True) * root
        row = jnp.sum(jnp.where(i == k, matrix, 0.0), axis=0, keepdims=True) * root
        row = jnp.where(lane >= k, row, 0.0)
        column = jnp.where(line > k, column, 0.0)
        lead = jnp.sum(jnp.where(i == k, inverse[...], 0.0), axis=0, keepdims=True) * root
        gram[...] = matrix - column * row
        inverse[...] = jnp.where(i == k, lead, inverse[...] - column * lead)
        factor[...] = jnp.where(i == k, row, factor[...])
        return carry

    lax.fori_loop(0, size, step, 0)


def improved(error, weight):
    lower = error * weight
    rounded = terms(lower, 1)
    return weight * product(rounded, rounded, NT) + (product(rounded, rounded) - lower)


def factor_kernel(lines, mine, theirs, solved, panel, factor, gram_ref, inverse_ref, factor_ref, panel_ref, sems):
    half = mine.shape[1]
    size = 2 * half
    lead = lax.axis_index("sec") == turned(lines) if lines else True
    block = jnp.where(lead, mine[:half, :], theirs[:half, :])
    corner = jnp.where(lead, theirs[:half, :], mine[:half, :])
    diagonal = jnp.where(lead, theirs[half : half + 1, :], mine[half : half + 1, :])
    i, j = grids(half, half)
    mirrored = corner.T
    gram_ref[:half, :half] = jnp.where(i >= j, corner, mirrored)
    gram_ref[half:, half:] = jnp.where(i < j, corner, jnp.where(i == j, diagonal, mirrored))
    gram_ref[half:, :half] = block
    gram_ref[:half, half:] = block.T
    gram = gram_ref[...]

    i, j = grids(size, size)
    unit = jnp.where(i == j, 1.0, 0.0)
    weight = jnp.where(i > j, 1.0, jnp.where(i == j, 0.5, 0.0))
    spread = gram * unit
    row = lax.rsqrt(jnp.sum(spread, axis=0, keepdims=True))
    column = lax.rsqrt(jnp.sum(spread, axis=1, keepdims=True))
    scaled = gram * column * row
    scaleds = terms(scaled, 2)
    solveds = terms(solved[...] * row, 2)
    moves = [
        pltpu.make_async_copy(source, place, sems.at[k])
        for k, (source, place) in enumerate([(panel_ref, panel), (factor_ref, factor)])
    ]

    def attempt(trial):
        upper = product(trial, scaleds)
        near = product(solveds, trial, NT)
        error = product(terms(upper, 2), trial, NT) - unit
        step = terms(improved(error, weight), 2)
        upper = upper + product(step, terms(upper, 2), NN, 1)
        factor_ref[...] = jnp.where(i <= j, upper / row, 0.0)
        moves[1].start()
        panel_ref[...] = near + product(terms(near, 2), step, NT, 1)
        moves[0].start()
        last = trial[0].astype(jnp.float32) + product(step, trial)
        error = product(terms(upper, 2), terms(last, 2), NT, 1) - unit
        open_entries = jnp.sum(jnp.where(jnp.abs(error) < 3e-5, 0.0, 1.0))
        moves[0].wait()
        moves[1].wait()
        return last, open_entries > 0.0

    trial = unit - (scaled - unit) * weight
    error = coarse(product(terms(trial, 1), scaleds[:1]), trial, NT) - unit
    trial = trial + coarse(improved(error, weight), trial)
    trial, unsettled = attempt(terms(trial, 1))

    @pl.when(unsettled)
    def _():
        _, again = attempt(terms(trial, 1))

        @pl.when(again)
        def _():
            eliminate(gram_ref, inverse_ref, factor_ref)
            panel_ref[...] = exact(solved[...], inverse_ref[...], NT)
            for move in moves:
                move.start()
            for move in moves:
                move.wait()


def finish(lines, mine, theirs, solved):
    rows, size = solved.shape
    scratch = [pltpu.VMEM((size, size), jnp.float32)] * 3
    scratch += [pltpu.VMEM((rows, size), jnp.float32), pltpu.SemaphoreType.DMA((2,))]
    return call(
        functools.partial(factor_kernel, lines),
        [shape(rows, size), shape(size, size)],
        [VMEM, VMEM, VMEM],
        "factor",
        24 * 2 * size**3,
        scratch,
        HBM,
    )(mine, theirs, solved)


def paired(lines, masks):
    pairs = []
    for place in range(2 * lines):
        line, core = divmod(place, 2)
        odd = lambda value: sum(value >> bit & 1 for bit in turning(lines)) % 2
        mask = masks[core ^ odd(line)]
        pairs.append((place, place ^ 2 * mask ^ odd(mask)))
    return pairs


def swap_lines(piece, lines):
    bits = (lines - 1).bit_length()
    groups = [[1 << b, 2 << b, 3 << b] for b in range(0, bits - 1, 2)]
    turn = len(groups) // 2
    for one, two in zip(groups, groups[turn:] + groups[:turn]):
        a, b, c = (lax.ppermute(piece, AXES, paired(lines, masks)) for masks in zip(one, two))
        piece = (piece + a) + (b + c)
    if bits % 2:
        mask = 1 << bits - 1
        piece = piece + lax.ppermute(piece, AXES, paired(lines, (mask, mask)))
    return piece


def two_sections(target, inverse, coupled, links, lines):
    rows, width = target.shape
    half = width // 2
    own = call(
        front_kernel,
        [shape(rows + inverse.shape[0], width)],
        [HBM, HBM, HBM, HBM],
        "front",
        4 * rows * rows * width,
        [
            pltpu.SMEM(links.shape, jnp.int32),
            pltpu.VMEM(target.shape, jnp.float32),
            pltpu.VMEM(inverse.shape, jnp.float32),
            pltpu.VMEM(coupled.shape, jnp.float32),
            pltpu.SemaphoreType.DMA((4,)),
        ],
    )(*(fetched(x) for x in (links, target, inverse, coupled)))[0]
    swap = [(0, 1), (1, 0)]
    other = lax.ppermute(own, "sec", swap)
    scale = 1.0 / (2 * lines * rows)
    solved, piece = call(
        functools.partial(gram_kernel, lines, scale),
        [shape(rows, width), shape(half + 8, half)],
        [VMEM, VMEM],
        "gram",
        6 * rows * rows * width,
    )(own, other)
    piece = swap_lines(piece, lines)
    theirs = lax.ppermute(piece, "sec", swap)
    return finish(lines, piece, theirs, solved)


def many_sections(target, inverse, coupled, links):
    section = lax.axis_index("sec")
    count = lax.axis_size("sec")
    acc = target
    solved = jnp.zeros_like(target)
    for anchor in range(count):
        mine = section == anchor
        candidate = jnp.where(mine, highest(inverse, acc), 0.0)
        arrived = lax.psum(candidate, "sec")
        solved = jnp.where(mine, arrived, solved)
        matrix = jnp.zeros_like(inverse)
        for slot in range(coupled.shape[0]):
            matrix = matrix + jnp.where(links[slot] == anchor, coupled[slot], 0.0)
        acc = acc - highest(matrix, arrived)
    total = lax.axis_size("line") * count * target.shape[0]
    gram = lax.psum(highest(solved, solved, TN), AXES) / total
    half = target.shape[1] // 2
    block, corner, diagonal = packed(gram, half)
    rest = jnp.broadcast_to(diagonal, (8, half))
    return finish(0, jnp.concatenate([block, rest]), jnp.concatenate([corner, rest]), solved)


def shards(right_side, inverse_diag, couplings, neighbors):
    local = (right_side[0, 0], inverse_diag[0, 0], couplings[0, 0], neighbors[0, 0])
    lines = lax.axis_size("line")
    if lax.axis_size("sec") == 2 and lines & (lines - 1) == 0:
        panel, factor = two_sections(*local, lines)
    else:
        panel, factor = many_sections(*local)
    return (panel[None, None], factor)


def solution(mesh):
    placed = (
        P("line", "sec", None, None),
        P("line", "sec", None, None),
        P("line", "sec", None, None, None),
        P("line", "sec", None),
    )
    return jax.shard_map(
        shards,
        mesh=mesh,
        in_specs=placed,
        out_specs=(P("line", "sec", None, None), P()),
        check_vma=False,
    )
```

```python
import functools

import jax
import jax.numpy as jnp
from jax import lax
from jax.experimental import pallas as pl
from jax.experimental.pallas import tpu as pltpu
from jax.sharding import PartitionSpec as P


AXES = ("line", "sec")
VMEM = pl.BlockSpec(memory_space=pltpu.VMEM)
HBM = pl.BlockSpec(memory_space=pltpu.HBM)
NN = (((1,), (0,)), ((), ()))
NT = (((1,), (1,)), ((), ()))
TN = (((0,), (0,)), ((), ()))


def terms(value, count=3):
    parts = []
    for _ in range(count):
        parts.append(value.astype(jnp.bfloat16))
        value = value - parts[-1].astype(jnp.float32)
    return parts


def product(left, right, dims=NN, order=2):
    total = None
    for level in range(order, -1, -1):
        for i in range(len(left)):
            if 0 <= level - i < len(right):
                part = lax.dot_general(
                    left[i], right[level - i], dims, preferred_element_type=jnp.float32
                )
                total = part if total is None else total + part
    return total


def exact(left, right, dims=NN):
    return product(terms(left), terms(right), dims)


def coarse(left, right, dims=NN):
    return product(terms(left, 1), terms(right, 1), dims)


def highest(left, right, dims=NN):
    return lax.dot_general(
        left, right, dims, precision=lax.Precision.HIGHEST, preferred_element_type=jnp.float32
    )


def call(kernel, outs, specs, name, flops, scratch=(), place=VMEM):
    moved = sum(4 * out.size for out in outs)
    return pl.pallas_call(
        kernel,
        out_shape=outs,
        in_specs=specs,
        out_specs=[place] * len(outs),
        scratch_shapes=list(scratch),
        compiler_params=pltpu.CompilerParams(vmem_limit_bytes=16 << 20),
        cost_estimate=pl.CostEstimate(flops=flops, bytes_accessed=moved, transcendentals=0),
        name=name,
    )


def fetched(value):
    return pltpu.with_memory_space_constraint(value, pltpu.HBM)


def shape(*dims):
    return jax.ShapeDtypeStruct(dims, jnp.float32)


def grids(rows, cols):
    return (
        lax.broadcasted_iota(jnp.int32, (rows, cols), 0),
        lax.broadcasted_iota(jnp.int32, (rows, cols), 1),
    )


def front_kernel(links, target, inverse, coupled, out, chosen, right, left, blocks, sems):
    rows = right.shape[0]
    moves = [
        pltpu.make_async_copy(source, place, sems.at[k])
        for k, (source, place) in enumerate(
            [(inverse, left), (target, right), (links, chosen), (coupled, blocks)]
        )
    ]
    for move in moves:
        move.start()
    for move in moves:
        move.wait()
    matrix = jnp.zeros(left.shape, jnp.float32)
    for slot in range(blocks.shape[0]):
        matrix = matrix + jnp.where(chosen[slot] >= 0, blocks[slot], 0.0)
    both = jnp.concatenate([right[...], matrix], axis=1)
    both = product(terms(left[...], 2), terms(both, 2), NN, 1)
    out[:rows, :] = both[:, : right.shape[1]]
    out[rows:, :] = both[:, right.shape[1] :]


def packed(gram, half):
    i, j = grids(half, half)
    last = gram[half:, half:]
    corner = jnp.where(i >= j, gram[:half, :half], last)
    diagonal = jnp.sum(jnp.where(i == j, last, 0.0), axis=0, keepdims=True)
    return gram[half:, :half], corner, diagonal


def turned(count):
    line = lax.axis_index("line")
    return sum((line >> bit) & 1 for bit in turning(count)) % 2


def turning(count):
    return sorted({0, max((count - 1).bit_length() - 1, 0)})


def gram_kernel(lines, scale, own, other, solved, piece):
    rows = own.shape[0] // 2
    half = own.shape[1] // 2
    section = lax.axis_index("sec")
    lead = section == 0
    first = jnp.where(lead, own[:rows, :], other[:rows, :])
    base = jnp.where(lead, other[:rows, :], own[:rows, :])
    carry = jnp.where(lead, other[rows:, :], own[rows:, :])
    firsts = terms(first, 2)
    second = base - product(terms(carry, 2), firsts, NN, 1)
    solved[...] = jnp.where(lead, first, second)
    seconds = terms(second, 2)
    gram = (product(firsts, firsts, TN) + product(seconds, seconds, TN)) * scale
    block, corner, diagonal = packed(gram, half)
    piece[:half, :] = jnp.where(section == turned(lines), block, corner)
    piece[half:, :] = jnp.broadcast_to(diagonal, (piece.shape[0] - half, half))


def eliminate(gram, inverse, factor):
    size = gram.shape[0]
    i, j = grids(size, size)
    inverse[...] = jnp.where(i == j, 1.0, 0.0)
    factor[...] = jnp.zeros_like(factor)
    lane = lax.broadcasted_iota(jnp.int32, (1, size), 1)
    line = lax.broadcasted_iota(jnp.int32, (size, 1), 0)

    def step(k, carry):
        matrix = gram[...]
        pivot = jnp.sum(jnp.where((i == k) & (j == k), matrix, 0.0), axis=(0, 1), keepdims=True)
        root = lax.rsqrt(pivot)
        root = root * (1.5 - 0.5 * pivot * root * root)
        column = jnp.sum(jnp.where(j == k, matrix, 0.0), axis=1, keepdims=True) * root
        row = jnp.sum(jnp.where(i == k, matrix, 0.0), axis=0, keepdims=True) * root
        row = jnp.where(lane >= k, row, 0.0)
        column = jnp.where(line > k, column, 0.0)
        lead = jnp.sum(jnp.where(i == k, inverse[...], 0.0), axis=0, keepdims=True) * root
        gram[...] = matrix - column * row
        inverse[...] = jnp.where(i == k, lead, inverse[...] - column * lead)
        factor[...] = jnp.where(i == k, row, factor[...])
        return carry

    lax.fori_loop(0, size, step, 0)


def improved(error, weight):
    lower = error * weight
    rounded = terms(lower, 1)
    return weight * product(rounded, rounded, NT) + (product(rounded, rounded) - lower)


def factor_kernel(lines, mine, theirs, solved, panel, factor, gram_ref, inverse_ref, factor_ref, panel_ref, sems):
    half = mine.shape[1]
    size = 2 * half
    lead = lax.axis_index("sec") == turned(lines) if lines else True
    block = jnp.where(lead, mine[:half, :], theirs[:half, :])
    corner = jnp.where(lead, theirs[:half, :], mine[:half, :])
    diagonal = jnp.where(lead, theirs[half : half + 1, :], mine[half : half + 1, :])
    i, j = grids(half, half)
    mirrored = corner.T
    gram_ref[:half, :half] = jnp.where(i >= j, corner, mirrored)
    gram_ref[half:, half:] = jnp.where(i < j, corner, jnp.where(i == j, diagonal, mirrored))
    gram_ref[half:, :half] = block
    gram_ref[:half, half:] = block.T
    gram = gram_ref[...]

    i, j = grids(size, size)
    unit = jnp.where(i == j, 1.0, 0.0)
    weight = jnp.where(i > j, 1.0, jnp.where(i == j, 0.5, 0.0))
    spread = gram * unit
    row = lax.rsqrt(jnp.sum(spread, axis=0, keepdims=True))
    column = lax.rsqrt(jnp.sum(spread, axis=1, keepdims=True))
    scaled = gram * column * row
    scaleds = terms(scaled, 2)
    solveds = terms(solved[...] * row, 2)
    moves = [
        pltpu.make_async_copy(source, place, sems.at[k])
        for k, (source, place) in enumerate([(panel_ref, panel), (factor_ref, factor)])
    ]

    def attempt(trial):
        upper = product(trial, scaleds)
        near = product(solveds, trial, NT)
        error = product(terms(upper, 2), trial, NT) - unit
        step = terms(improved(error, weight), 2)
        upper = upper + product(step, terms(upper, 2), NN, 1)
        factor_ref[...] = jnp.where(i <= j, upper / row, 0.0)
        moves[1].start()
        panel_ref[...] = near + product(terms(near, 2), step, NT, 1)
        moves[0].start()
        last = trial[0].astype(jnp.float32) + product(step, trial)
        error = product(terms(upper, 2), terms(last, 2), NT, 1) - unit
        open_entries = jnp.sum(jnp.where(jnp.abs(error) < 3e-5, 0.0, 1.0))
        moves[0].wait()
        moves[1].wait()
        return last, open_entries > 0.0

    trial = unit - (scaled - unit) * weight
    error = coarse(product(terms(trial, 1), scaleds[:1]), trial, NT) - unit
    trial = trial + coarse(improved(error, weight), trial)
    trial, unsettled = attempt(terms(trial, 1))

    @pl.when(unsettled)
    def _():
        _, again = attempt(terms(trial, 1))

        @pl.when(again)
        def _():
            eliminate(gram_ref, inverse_ref, factor_ref)
            panel_ref[...] = exact(solved[...], inverse_ref[...], NT)
            for move in moves:
                move.start()
            for move in moves:
                move.wait()


def finish(lines, mine, theirs, solved):
    rows, size = solved.shape
    scratch = [pltpu.VMEM((size, size), jnp.float32)] * 3
    scratch += [pltpu.VMEM((rows, size), jnp.float32), pltpu.SemaphoreType.DMA((2,))]
    return call(
        functools.partial(factor_kernel, lines),
        [shape(rows, size), shape(size, size)],
        [VMEM, VMEM, VMEM],
        "factor",
        24 * 2 * size**3,
        scratch,
        HBM,
    )(mine, theirs, solved)


def paired(lines, masks):
    pairs = []
    for place in range(2 * lines):
        line, core = divmod(place, 2)
        odd = lambda value: sum(value >> bit & 1 for bit in turning(lines)) % 2
        mask = masks[core ^ odd(line)]
        pairs.append((place, place ^ 2 * mask ^ odd(mask)))
    return pairs


def swap_lines(piece, lines):
    bits = (lines - 1).bit_length()
    groups = [[2 << b, 1 << b, 3 << b] for b in range(0, bits - 1, 2)]
    turn = len(groups) // 2
    for one, two in zip(groups, groups[turn:] + groups[:turn]):
        a, b, c = (lax.ppermute(piece, AXES, paired(lines, masks)) for masks in zip(one, two))
        piece = (piece + a) + (b + c)
    if bits % 2:
        mask = 1 << bits - 1
        piece = piece + lax.ppermute(piece, AXES, paired(lines, (mask, mask)))
    return piece


def two_sections(target, inverse, coupled, links, lines):
    rows, width = target.shape
    half = width // 2
    own = call(
        front_kernel,
        [shape(rows + inverse.shape[0], width)],
        [HBM, HBM, HBM, HBM],
        "front",
        4 * rows * rows * width,
        [
            pltpu.SMEM(links.shape, jnp.int32),
            pltpu.VMEM(target.shape, jnp.float32),
            pltpu.VMEM(inverse.shape, jnp.float32),
            pltpu.VMEM(coupled.shape, jnp.float32),
            pltpu.SemaphoreType.DMA((4,)),
        ],
    )(*(fetched(x) for x in (links, target, inverse, coupled)))[0]
    swap = [(0, 1), (1, 0)]
    other = lax.ppermute(own, "sec", swap)
    scale = 1.0 / (2 * lines * rows)
    solved, piece = call(
        functools.partial(gram_kernel, lines, scale),
        [shape(rows, width), shape(half + 8, half)],
        [VMEM, VMEM],
        "gram",
        6 * rows * rows * width,
    )(own, other)
    piece = swap_lines(piece, lines)
    theirs = lax.ppermute(piece, "sec", swap)
    return finish(lines, piece, theirs, solved)


def many_sections(target, inverse, coupled, links):
    section = lax.axis_index("sec")
    count = lax.axis_size("sec")
    acc = target
    solved = jnp.zeros_like(target)
    for anchor in range(count):
        mine = section == anchor
        candidate = jnp.where(mine, highest(inverse, acc), 0.0)
        arrived = lax.psum(candidate, "sec")
        solved = jnp.where(mine, arrived, solved)
        matrix = jnp.zeros_like(inverse)
        for slot in range(coupled.shape[0]):
            matrix = matrix + jnp.where(links[slot] == anchor, coupled[slot], 0.0)
        acc = acc - highest(matrix, arrived)
    total = lax.axis_size("line") * count * target.shape[0]
    gram = lax.psum(highest(solved, solved, TN), AXES) / total
    half = target.shape[1] // 2
    block, corner, diagonal = packed(gram, half)
    rest = jnp.broadcast_to(diagonal, (8, half))
    return finish(0, jnp.concatenate([block, rest]), jnp.concatenate([corner, rest]), solved)


def shards(right_side, inverse_diag, couplings, neighbors):
    local = (right_side[0, 0], inverse_diag[0, 0], couplings[0, 0], neighbors[0, 0])
    lines = lax.axis_size("line")
    if lax.axis_size("sec") == 2 and lines & (lines - 1) == 0:
        panel, factor = two_sections(*local, lines)
    else:
        panel, factor = many_sections(*local)
    return (panel[None, None], factor)


def solution(mesh):
    placed = (
        P("line", "sec", None, None),
        P("line", "sec", None, None),
        P("line", "sec", None, None, None),
        P("line", "sec", None),
    )
    return jax.shard_map(
        shards,
        mesh=mesh,
        in_specs=placed,
        out_specs=(P("line", "sec", None, None), P()),
        check_vma=False,
    )
```

```python
import functools

import jax
import jax.numpy as jnp
from jax import lax
from jax.experimental import pallas as pl
from jax.experimental.pallas import tpu as pltpu
from jax.sharding import PartitionSpec as P


AXES = ("line", "sec")
VMEM = pl.BlockSpec(memory_space=pltpu.VMEM)
HBM = pl.BlockSpec(memory_space=pltpu.HBM)
NN = (((1,), (0,)), ((), ()))
NT = (((1,), (1,)), ((), ()))
TN = (((0,), (0,)), ((), ()))


def terms(value, count=3):
    parts = []
    for _ in range(count):
        parts.append(value.astype(jnp.bfloat16))
        value = value - parts[-1].astype(jnp.float32)
    return parts


def product(left, right, dims=NN, order=2):
    total = None
    for level in range(order, -1, -1):
        for i in range(len(left)):
            if 0 <= level - i < len(right):
                part = lax.dot_general(
                    left[i], right[level - i], dims, preferred_element_type=jnp.float32
                )
                total = part if total is None else total + part
    return total


def exact(left, right, dims=NN):
    return product(terms(left), terms(right), dims)


def coarse(left, right, dims=NN):
    return product(terms(left, 1), terms(right, 1), dims)


def highest(left, right, dims=NN):
    return lax.dot_general(
        left, right, dims, precision=lax.Precision.HIGHEST, preferred_element_type=jnp.float32
    )


def call(kernel, outs, specs, name, flops, scratch=(), place=VMEM):
    moved = sum(4 * out.size for out in outs)
    return pl.pallas_call(
        kernel,
        out_shape=outs,
        in_specs=specs,
        out_specs=[place] * len(outs),
        scratch_shapes=list(scratch),
        compiler_params=pltpu.CompilerParams(vmem_limit_bytes=16 << 20),
        cost_estimate=pl.CostEstimate(flops=flops, bytes_accessed=moved, transcendentals=0),
        name=name,
    )


def fetched(value):
    return pltpu.with_memory_space_constraint(value, pltpu.HBM)


def shape(*dims):
    return jax.ShapeDtypeStruct(dims, jnp.float32)


def grids(rows, cols):
    return (
        lax.broadcasted_iota(jnp.int32, (rows, cols), 0),
        lax.broadcasted_iota(jnp.int32, (rows, cols), 1),
    )


def front_kernel(links, target, inverse, coupled, base, carry, chosen, right, left, blocks, sems):
    moves = [
        pltpu.make_async_copy(source, place, sems.at[k])
        for k, (source, place) in enumerate(
            [(inverse, left), (target, right), (links, chosen), (coupled, blocks)]
        )
    ]
    for move in moves:
        move.start()
    for move in moves:
        move.wait()
    matrix = jnp.zeros(left.shape, jnp.float32)
    for slot in range(blocks.shape[0]):
        matrix = matrix + jnp.where(chosen[slot] >= 0, blocks[slot], 0.0)
    both = jnp.concatenate([right[...], matrix], axis=1)
    both = product(terms(left[...], 2), terms(both, 2), NN, 1)
    base[...] = both[:, : right.shape[1]]
    carry[...] = both[:, right.shape[1] :]


def packed(gram, half):
    i, j = grids(half, half)
    last = gram[half:, half:]
    corner = jnp.where(i >= j, gram[:half, :half], last)
    diagonal = jnp.sum(jnp.where(i == j, last, 0.0), axis=0, keepdims=True)
    return gram[half:, :half], corner, diagonal


def turned(count):
    line = lax.axis_index("line")
    return sum((line >> bit) & 1 for bit in turning(count)) % 2


def turning(count):
    return sorted({0, max((count - 1).bit_length() - 1, 0)})


def gram_kernel(lines, scale, base0, carry0, base1, carry1, solved, piece):
    half = base0.shape[1] // 2
    section = lax.axis_index("sec")
    lead = section == 0
    first = jnp.where(lead, base0[...], base1[...])
    base = jnp.where(lead, base1[...], base0[...])
    carry = jnp.where(lead, carry1[...], carry0[...])
    firsts = terms(first, 2)
    second = base - product(terms(carry, 2), firsts, NN, 1)
    solved[...] = jnp.where(lead, first, second)
    seconds = terms(second, 2)
    gram = (product(firsts, firsts, TN, 1) + product(seconds, seconds, TN, 1)) * scale
    block, corner, diagonal = packed(gram, half)
    piece[:half, :] = jnp.where(section == turned(lines), block, corner)
    piece[half:, :] = jnp.broadcast_to(diagonal, (piece.shape[0] - half, half))


def eliminate(gram, inverse, factor):
    size = gram.shape[0]
    i, j = grids(size, size)
    inverse[...] = jnp.where(i == j, 1.0, 0.0)
    factor[...] = jnp.zeros_like(factor)
    lane = lax.broadcasted_iota(jnp.int32, (1, size), 1)
    line = lax.broadcasted_iota(jnp.int32, (size, 1), 0)

    def step(k, carry):
        matrix = gram[...]
        pivot = jnp.sum(jnp.where((i == k) & (j == k), matrix, 0.0), axis=(0, 1), keepdims=True)
        root = lax.rsqrt(pivot)
        root = root * (1.5 - 0.5 * pivot * root * root)
        column = jnp.sum(jnp.where(j == k, matrix, 0.0), axis=1, keepdims=True) * root
        row = jnp.sum(jnp.where(i == k, matrix, 0.0), axis=0, keepdims=True) * root
        row = jnp.where(lane >= k, row, 0.0)
        column = jnp.where(line > k, column, 0.0)
        lead = jnp.sum(jnp.where(i == k, inverse[...], 0.0), axis=0, keepdims=True) * root
        gram[...] = matrix - column * row
        inverse[...] = jnp.where(i == k, lead, inverse[...] - column * lead)
        factor[...] = jnp.where(i == k, row, factor[...])
        return carry

    lax.fori_loop(0, size, step, 0)


def improved(error, weight):
    lower = error * weight
    rounded = terms(lower, 1)
    return weight * product(rounded, rounded, NT) + (product(rounded, rounded) - lower)


def factor_kernel(lines, mine, theirs, solved, panel, factor, gram_ref, inverse_ref, factor_ref, panel_ref, sems):
    half = mine.shape[1]
    size = 2 * half
    lead = lax.axis_index("sec") == turned(lines) if lines else True
    block = jnp.where(lead, mine[:half, :], theirs[:half, :])
    corner = jnp.where(lead, theirs[:half, :], mine[:half, :])
    diagonal = jnp.where(lead, theirs[half : half + 1, :], mine[half : half + 1, :])
    i, j = grids(half, half)
    mirrored = corner.T
    gram_ref[:half, :half] = jnp.where(i >= j, corner, mirrored)
    gram_ref[half:, half:] = jnp.where(i < j, corner, jnp.where(i == j, diagonal, mirrored))
    gram_ref[half:, :half] = block
    gram_ref[:half, half:] = block.T
    gram = gram_ref[...]

    i, j = grids(size, size)
    unit = jnp.where(i == j, 1.0, 0.0)
    weight = jnp.where(i > j, 1.0, jnp.where(i == j, 0.5, 0.0))
    spread = gram * unit
    row = lax.rsqrt(jnp.sum(spread, axis=0, keepdims=True))
    column = lax.rsqrt(jnp.sum(spread, axis=1, keepdims=True))
    scaled = gram * column * row
    scaleds = terms(scaled, 2)
    solveds = terms(solved[...] * row, 2)
    moves = [
        pltpu.make_async_copy(source, place, sems.at[k])
        for k, (source, place) in enumerate([(panel_ref, panel), (factor_ref, factor)])
    ]

    def attempt(trial):
        upper = product(trial, scaleds)
        near = product(solveds, trial, NT)
        error = product(terms(upper, 2), trial, NT) - unit
        step = terms(improved(error, weight), 2)
        upper = upper + product(step, terms(upper, 2), NN, 1)
        factor_ref[...] = jnp.where(i <= j, upper / row, 0.0)
        moves[1].start()
        panel_ref[...] = near + product(terms(near, 2), step, NT, 1)
        moves[0].start()
        last = trial[0].astype(jnp.float32) + product(step, trial)
        error = product(terms(upper, 2), terms(last, 2), NT, 1) - unit
        open_entries = jnp.sum(jnp.where(jnp.abs(error) < 3e-5, 0.0, 1.0))
        moves[0].wait()
        moves[1].wait()
        return last, open_entries > 0.0

    trial = unit - (scaled - unit) * weight
    error = coarse(product(terms(trial, 1), scaleds[:1]), trial, NT) - unit
    trial = trial + coarse(improved(error, weight), trial)
    trial, unsettled = attempt(terms(trial, 1))

    @pl.when(unsettled)
    def _():
        _, again = attempt(terms(trial, 1))

        @pl.when(again)
        def _():
            eliminate(gram_ref, inverse_ref, factor_ref)
            panel_ref[...] = exact(solved[...], inverse_ref[...], NT)
            for move in moves:
                move.start()
            for move in moves:
                move.wait()


def finish(lines, mine, theirs, solved):
    rows, size = solved.shape
    scratch = [pltpu.VMEM((size, size), jnp.float32)] * 3
    scratch += [pltpu.VMEM((rows, size), jnp.float32), pltpu.SemaphoreType.DMA((2,))]
    return call(
        functools.partial(factor_kernel, lines),
        [shape(rows, size), shape(size, size)],
        [VMEM, VMEM, VMEM],
        "factor",
        24 * 2 * size**3,
        scratch,
        HBM,
    )(mine, theirs, solved)


def paired(lines, masks):
    pairs = []
    for place in range(2 * lines):
        line, core = divmod(place, 2)
        odd = lambda value: sum(value >> bit & 1 for bit in turning(lines)) % 2
        mask = masks[core ^ odd(line)]
        pairs.append((place, place ^ 2 * mask ^ odd(mask)))
    return pairs


def swap_lines(piece, lines):
    bits = (lines - 1).bit_length()
    groups = [[2 << b, 1 << b, 3 << b] for b in range(0, bits - 1, 2)]
    turn = len(groups) // 2
    for one, two in zip(groups, groups[turn:] + groups[:turn]):
        a, b, c = (lax.ppermute(piece, AXES, paired(lines, masks)) for masks in zip(one, two))
        piece = (piece + a) + (b + c)
    if bits % 2:
        mask = 1 << bits - 1
        piece = piece + lax.ppermute(piece, AXES, paired(lines, (mask, mask)))
    return piece


def two_sections(target, inverse, coupled, links, lines):
    rows, width = target.shape
    half = width // 2
    own = call(
        front_kernel,
        [shape(rows, width), shape(*inverse.shape)],
        [HBM, HBM, HBM, HBM],
        "front",
        4 * rows * rows * width,
        [
            pltpu.SMEM(links.shape, jnp.int32),
            pltpu.VMEM(target.shape, jnp.float32),
            pltpu.VMEM(inverse.shape, jnp.float32),
            pltpu.VMEM(coupled.shape, jnp.float32),
            pltpu.SemaphoreType.DMA((4,)),
        ],
    )(*(fetched(x) for x in (links, target, inverse, coupled)))
    swap = [(0, 1), (1, 0)]
    other = [lax.ppermute(x, "sec", swap) for x in own]
    scale = 1.0 / (2 * lines * rows)
    solved, piece = call(
        functools.partial(gram_kernel, lines, scale),
        [shape(rows, width), shape(half + 8, half)],
        [VMEM, VMEM, VMEM, VMEM],
        "gram",
        6 * rows * rows * width,
    )(*own, *other)
    piece = swap_lines(piece, lines)
    theirs = lax.ppermute(piece, "sec", swap)
    return finish(lines, piece, theirs, solved)


def many_sections(target, inverse, coupled, links):
    section = lax.axis_index("sec")
    count = lax.axis_size("sec")
    acc = target
    solved = jnp.zeros_like(target)
    for anchor in range(count):
        mine = section == anchor
        candidate = jnp.where(mine, highest(inverse, acc), 0.0)
        arrived = lax.psum(candidate, "sec")
        solved = jnp.where(mine, arrived, solved)
        matrix = jnp.zeros_like(inverse)
        for slot in range(coupled.shape[0]):
            matrix = matrix + jnp.where(links[slot] == anchor, coupled[slot], 0.0)
        acc = acc - highest(matrix, arrived)
    total = lax.axis_size("line") * count * target.shape[0]
    gram = lax.psum(highest(solved, solved, TN), AXES) / total
    half = target.shape[1] // 2
    block, corner, diagonal = packed(gram, half)
    rest = jnp.broadcast_to(diagonal, (8, half))
    return finish(0, jnp.concatenate([block, rest]), jnp.concatenate([corner, rest]), solved)


def shards(right_side, inverse_diag, couplings, neighbors):
    local = (right_side[0, 0], inverse_diag[0, 0], couplings[0, 0], neighbors[0, 0])
    lines = lax.axis_size("line")
    if lax.axis_size("sec") == 2 and lines & (lines - 1) == 0:
        panel, factor = two_sections(*local, lines)
    else:
        panel, factor = many_sections(*local)
    return (panel[None, None], factor)


def solution(mesh):
    placed = (
        P("line", "sec", None, None),
        P("line", "sec", None, None),
        P("line", "sec", None, None, None),
        P("line", "sec", None),
    )
    return jax.shard_map(
        shards,
        mesh=mesh,
        in_specs=placed,
        out_specs=(P("line", "sec", None, None), P()),
        check_vma=False,
    )
```

```python
import functools

import jax
import jax.numpy as jnp
from jax import lax
from jax.experimental import pallas as pl
from jax.experimental.pallas import tpu as pltpu
from jax.sharding import PartitionSpec as P


AXES = ("line", "sec")
VMEM = pl.BlockSpec(memory_space=pltpu.VMEM)
HBM = pl.BlockSpec(memory_space=pltpu.HBM)
NN = (((1,), (0,)), ((), ()))
NT = (((1,), (1,)), ((), ()))
TN = (((0,), (0,)), ((), ()))


def terms(value, count=3):
    parts = []
    for _ in range(count):
        parts.append(value.astype(jnp.bfloat16))
        value = value - parts[-1].astype(jnp.float32)
    return parts


def product(left, right, dims=NN, order=2):
    total = None
    for level in range(order, -1, -1):
        for i in range(len(left)):
            if 0 <= level - i < len(right):
                part = lax.dot_general(
                    left[i], right[level - i], dims, preferred_element_type=jnp.float32
                )
                total = part if total is None else total + part
    return total


def exact(left, right, dims=NN):
    return product(terms(left), terms(right), dims)


def coarse(left, right, dims=NN):
    return product(terms(left, 1), terms(right, 1), dims)


def highest(left, right, dims=NN):
    return lax.dot_general(
        left, right, dims, precision=lax.Precision.HIGHEST, preferred_element_type=jnp.float32
    )


def call(kernel, outs, specs, name, flops, scratch=(), place=VMEM):
    moved = sum(4 * out.size for out in outs)
    return pl.pallas_call(
        kernel,
        out_shape=outs,
        in_specs=specs,
        out_specs=[place] * len(outs),
        scratch_shapes=list(scratch),
        compiler_params=pltpu.CompilerParams(vmem_limit_bytes=16 << 20),
        cost_estimate=pl.CostEstimate(flops=flops, bytes_accessed=moved, transcendentals=0),
        name=name,
    )


def fetched(value):
    return pltpu.with_memory_space_constraint(value, pltpu.HBM)


def shape(*dims):
    return jax.ShapeDtypeStruct(dims, jnp.float32)


def grids(rows, cols):
    return (
        lax.broadcasted_iota(jnp.int32, (rows, cols), 0),
        lax.broadcasted_iota(jnp.int32, (rows, cols), 1),
    )


def front_kernel(links, target, inverse, coupled, out, chosen, right, left, blocks, sems):
    rows = right.shape[0]
    moves = [
        pltpu.make_async_copy(source, place, sems.at[k])
        for k, (source, place) in enumerate(
            [(inverse, left), (target, right), (links, chosen), (coupled, blocks)]
        )
    ]
    for move in moves:
        move.start()
    for move in moves:
        move.wait()
    matrix = jnp.zeros(left.shape, jnp.float32)
    for slot in range(blocks.shape[0]):
        matrix = matrix + jnp.where(chosen[slot] >= 0, blocks[slot], 0.0)
    both = jnp.concatenate([right[...], matrix], axis=1)
    both = product(terms(left[...], 2), terms(both, 2), NN, 1)
    out[:rows, :] = both[:, : right.shape[1]]
    out[rows:, :] = both[:, right.shape[1] :]


def packed(gram, half):
    i, j = grids(half, half)
    last = gram[half:, half:]
    corner = jnp.where(i >= j, gram[:half, :half], last)
    diagonal = jnp.sum(jnp.where(i == j, last, 0.0), axis=0, keepdims=True)
    return gram[half:, :half], corner, diagonal


def turned(count):
    line = lax.axis_index("line")
    return sum((line >> bit) & 1 for bit in turning(count)) % 2


def turning(count):
    return sorted({0, max((count - 1).bit_length() - 1, 0)})


def gram_kernel(lines, scale, own, other, solved, piece):
    rows = own.shape[0] // 2
    half = own.shape[1] // 2
    section = lax.axis_index("sec")
    lead = section == 0
    first = jnp.where(lead, own[:rows, :], other[:rows, :])
    base = jnp.where(lead, other[:rows, :], own[:rows, :])
    carry = jnp.where(lead, other[rows:, :], own[rows:, :])
    firsts = terms(first, 2)
    second = base - product(terms(carry, 2), firsts, NN, 1)
    solved[...] = jnp.where(lead, first, second)
    seconds = terms(second, 2)
    gram = (product(firsts, firsts, TN) + product(seconds, seconds, TN)) * scale
    block, corner, diagonal = packed(gram, half)
    piece[:half, :] = jnp.where(section == turned(lines), block, corner)
    piece[half:, :] = jnp.broadcast_to(diagonal, (piece.shape[0] - half, half))


def eliminate(gram, inverse, factor):
    size = gram.shape[0]
    i, j = grids(size, size)
    inverse[...] = jnp.where(i == j, 1.0, 0.0)
    factor[...] = jnp.zeros_like(factor)
    lane = lax.broadcasted_iota(jnp.int32, (1, size), 1)
    line = lax.broadcasted_iota(jnp.int32, (size, 1), 0)

    def step(k, carry):
        matrix = gram[...]
        pivot = jnp.sum(jnp.where((i == k) & (j == k), matrix, 0.0), axis=(0, 1), keepdims=True)
        root = lax.rsqrt(pivot)
        root = root * (1.5 - 0.5 * pivot * root * root)
        column = jnp.sum(jnp.where(j == k, matrix, 0.0), axis=1, keepdims=True) * root
        row = jnp.sum(jnp.where(i == k, matrix, 0.0), axis=0, keepdims=True) * root
        row = jnp.where(lane >= k, row, 0.0)
        column = jnp.where(line > k, column, 0.0)
        lead = jnp.sum(jnp.where(i == k, inverse[...], 0.0), axis=0, keepdims=True) * root
        gram[...] = matrix - column * row
        inverse[...] = jnp.where(i == k, lead, inverse[...] - column * lead)
        factor[...] = jnp.where(i == k, row, factor[...])
        return carry

    lax.fori_loop(0, size, step, 0)


def improved(error, weight, unit):
    lower = error * weight
    return weight * coarse(lower, error) + (0.5 * unit * lower * lower - lower)


def factor_kernel(lines, mine, theirs, solved, panel, factor, gram_ref, inverse_ref, factor_ref, panel_ref, sems):
    half = mine.shape[1]
    size = 2 * half
    lead = lax.axis_index("sec") == turned(lines) if lines else True
    block = jnp.where(lead, mine[:half, :], theirs[:half, :])
    corner = jnp.where(lead, theirs[:half, :], mine[:half, :])
    diagonal = jnp.where(lead, theirs[half : half + 1, :], mine[half : half + 1, :])
    i, j = grids(half, half)
    mirrored = corner.T
    gram_ref[:half, :half] = jnp.where(i >= j, corner, mirrored)
    gram_ref[half:, half:] = jnp.where(i < j, corner, jnp.where(i == j, diagonal, mirrored))
    gram_ref[half:, :half] = block
    gram_ref[:half, half:] = block.T
    gram = gram_ref[...]

    i, j = grids(size, size)
    unit = jnp.where(i == j, 1.0, 0.0)
    weight = jnp.where(i > j, 1.0, jnp.where(i == j, 0.5, 0.0))
    spread = gram * unit
    row = lax.rsqrt(jnp.sum(spread, axis=0, keepdims=True))
    column = lax.rsqrt(jnp.sum(spread, axis=1, keepdims=True))
    scaled = gram * column * row
    scaleds = terms(scaled, 2)
    solveds = terms(solved[...] * row, 2)
    moves = [
        pltpu.make_async_copy(source, place, sems.at[k])
        for k, (source, place) in enumerate([(panel_ref, panel), (factor_ref, factor)])
    ]

    def attempt(trial):
        upper = product(trial, scaleds)
        near = product(solveds, trial, NT)
        error = product(terms(upper, 2), trial, NT) - unit
        step = terms(improved(error, weight, unit), 2)
        upper = upper + product(step, terms(upper, 2), NN, 1)
        factor_ref[...] = jnp.where(i <= j, upper / row, 0.0)
        moves[1].start()
        panel_ref[...] = near + product(terms(near, 2), step, NT, 1)
        moves[0].start()
        last = trial[0].astype(jnp.float32) + product(step, trial)
        error = product(terms(upper, 2), terms(last, 2), NT, 1) - unit
        open_entries = jnp.sum(jnp.where(jnp.abs(error) < 3e-5, 0.0, 1.0))
        moves[0].wait()
        moves[1].wait()
        return last, open_entries > 0.0

    trial = unit - (scaled - unit) * weight
    error = coarse(product(terms(trial, 1), scaleds[:1]), trial, NT) - unit
    trial = trial + coarse(improved(error, weight, unit), trial)
    trial, unsettled = attempt(terms(trial, 1))

    @pl.when(unsettled)
    def _():
        _, again = attempt(terms(trial, 1))

        @pl.when(again)
        def _():
            eliminate(gram_ref, inverse_ref, factor_ref)
            panel_ref[...] = exact(solved[...], inverse_ref[...], NT)
            for move in moves:
                move.start()
            for move in moves:
                move.wait()


def finish(lines, mine, theirs, solved):
    rows, size = solved.shape
    scratch = [pltpu.VMEM((size, size), jnp.float32)] * 3
    scratch += [pltpu.VMEM((rows, size), jnp.float32), pltpu.SemaphoreType.DMA((2,))]
    return call(
        functools.partial(factor_kernel, lines),
        [shape(rows, size), shape(size, size)],
        [VMEM, VMEM, VMEM],
        "factor",
        24 * 2 * size**3,
        scratch,
        HBM,
    )(mine, theirs, solved)


def paired(lines, masks):
    pairs = []
    for place in range(2 * lines):
        line, core = divmod(place, 2)
        odd = lambda value: sum(value >> bit & 1 for bit in turning(lines)) % 2
        mask = masks[core ^ odd(line)]
        pairs.append((place, place ^ 2 * mask ^ odd(mask)))
    return pairs


def swap_lines(piece, lines):
    bits = (lines - 1).bit_length()
    groups = [[2 << b, 1 << b, 3 << b] for b in range(0, bits - 1, 2)]
    turn = len(groups) // 2
    for one, two in zip(groups, groups[turn:] + groups[:turn]):
        a, b, c = (lax.ppermute(piece, AXES, paired(lines, masks)) for masks in zip(one, two))
        piece = (piece + a) + (b + c)
    if bits % 2:
        mask = 1 << bits - 1
        piece = piece + lax.ppermute(piece, AXES, paired(lines, (mask, mask)))
    return piece


def two_sections(target, inverse, coupled, links, lines):
    rows, width = target.shape
    half = width // 2
    own = call(
        front_kernel,
        [shape(rows + inverse.shape[0], width)],
        [HBM, HBM, HBM, HBM],
        "front",
        4 * rows * rows * width,
        [
            pltpu.SMEM(links.shape, jnp.int32),
            pltpu.VMEM(target.shape, jnp.float32),
            pltpu.VMEM(inverse.shape, jnp.float32),
            pltpu.VMEM(coupled.shape, jnp.float32),
            pltpu.SemaphoreType.DMA((4,)),
        ],
    )(*(fetched(x) for x in (links, target, inverse, coupled)))[0]
    swap = [(0, 1), (1, 0)]
    other = lax.ppermute(own, "sec", swap)
    scale = 1.0 / (2 * lines * rows)
    solved, piece = call(
        functools.partial(gram_kernel, lines, scale),
        [shape(rows, width), shape(half + 8, half)],
        [VMEM, VMEM],
        "gram",
        6 * rows * rows * width,
    )(own, other)
    piece = swap_lines(piece, lines)
    theirs = lax.ppermute(piece, "sec", swap)
    return finish(lines, piece, theirs, solved)


def many_sections(target, inverse, coupled, links):
    section = lax.axis_index("sec")
    count = lax.axis_size("sec")
    acc = target
    solved = jnp.zeros_like(target)
    for anchor in range(count):
        mine = section == anchor
        candidate = jnp.where(mine, highest(inverse, acc), 0.0)
        arrived = lax.psum(candidate, "sec")
        solved = jnp.where(mine, arrived, solved)
        matrix = jnp.zeros_like(inverse)
        for slot in range(coupled.shape[0]):
            matrix = matrix + jnp.where(links[slot] == anchor, coupled[slot], 0.0)
        acc = acc - highest(matrix, arrived)
    total = lax.axis_size("line") * count * target.shape[0]
    gram = lax.psum(highest(solved, solved, TN), AXES) / total
    half = target.shape[1] // 2
    block, corner, diagonal = packed(gram, half)
    rest = jnp.broadcast_to(diagonal, (8, half))
    return finish(0, jnp.concatenate([block, rest]), jnp.concatenate([corner, rest]), solved)


def shards(right_side, inverse_diag, couplings, neighbors):
    local = (right_side[0, 0], inverse_diag[0, 0], couplings[0, 0], neighbors[0, 0])
    lines = lax.axis_size("line")
    if lax.axis_size("sec") == 2 and lines & (lines - 1) == 0:
        panel, factor = two_sections(*local, lines)
    else:
        panel, factor = many_sections(*local)
    return (panel[None, None], factor)


def solution(mesh):
    placed = (
        P("line", "sec", None, None),
        P("line", "sec", None, None),
        P("line", "sec", None, None, None),
        P("line", "sec", None),
    )
    return jax.shard_map(
        shards,
        mesh=mesh,
        in_specs=placed,
        out_specs=(P("line", "sec", None, None), P()),
        check_vma=False,
    )
```

```python
import functools

import jax
import jax.numpy as jnp
from jax import lax
from jax.experimental import pallas as pl
from jax.experimental.pallas import tpu as pltpu
from jax.sharding import PartitionSpec as P


AXES = ("line", "sec")
VMEM = pl.BlockSpec(memory_space=pltpu.VMEM)
HBM = pl.BlockSpec(memory_space=pltpu.HBM)
NN = (((1,), (0,)), ((), ()))
NT = (((1,), (1,)), ((), ()))
TN = (((0,), (0,)), ((), ()))


def terms(value, count=3):
    parts = []
    for _ in range(count):
        parts.append(value.astype(jnp.bfloat16))
        value = value - parts[-1].astype(jnp.float32)
    return parts


def product(left, right, dims=NN, order=2):
    total = None
    for level in range(order, -1, -1):
        for i in range(len(left)):
            if 0 <= level - i < len(right):
                part = lax.dot_general(
                    left[i], right[level - i], dims, preferred_element_type=jnp.float32
                )
                total = part if total is None else total + part
    return total


def exact(left, right, dims=NN):
    return product(terms(left), terms(right), dims)


def coarse(left, right, dims=NN):
    return product(terms(left, 1), terms(right, 1), dims)


def highest(left, right, dims=NN):
    return lax.dot_general(
        left, right, dims, precision=lax.Precision.HIGHEST, preferred_element_type=jnp.float32
    )


def call(kernel, outs, specs, name, flops, scratch=(), place=VMEM):
    moved = sum(4 * out.size for out in outs)
    return pl.pallas_call(
        kernel,
        out_shape=outs,
        in_specs=specs,
        out_specs=[place] * len(outs),
        scratch_shapes=list(scratch),
        compiler_params=pltpu.CompilerParams(vmem_limit_bytes=16 << 20),
        cost_estimate=pl.CostEstimate(flops=flops, bytes_accessed=moved, transcendentals=0),
        name=name,
    )


def fetched(value):
    return pltpu.with_memory_space_constraint(value, pltpu.HBM)


def shape(*dims):
    return jax.ShapeDtypeStruct(dims, jnp.float32)


def grids(rows, cols):
    return (
        lax.broadcasted_iota(jnp.int32, (rows, cols), 0),
        lax.broadcasted_iota(jnp.int32, (rows, cols), 1),
    )


def front_kernel(links, target, inverse, coupled, out, chosen, right, left, blocks, sems):
    rows = right.shape[0]
    moves = [
        pltpu.make_async_copy(source, place, sems.at[k])
        for k, (source, place) in enumerate(
            [(inverse, left), (target, right), (links, chosen), (coupled, blocks)]
        )
    ]
    for move in moves:
        move.start()
    for move in moves:
        move.wait()
    matrix = jnp.zeros(left.shape, jnp.float32)
    for slot in range(blocks.shape[0]):
        matrix = matrix + jnp.where(chosen[slot] >= 0, blocks[slot], 0.0)
    both = jnp.concatenate([right[...], matrix], axis=1)
    both = product(terms(left[...], 2), terms(both, 2), NN, 1)
    out[:rows, :] = both[:, : right.shape[1]]
    out[rows:, :] = both[:, right.shape[1] :]


def packed(gram, half):
    i, j = grids(half, half)
    last = gram[half:, half:]
    corner = jnp.where(i >= j, gram[:half, :half], last)
    diagonal = jnp.sum(jnp.where(i == j, last, 0.0), axis=0, keepdims=True)
    return gram[half:, :half], corner, diagonal


def turned(count):
    line = lax.axis_index("line")
    return sum((line >> bit) & 1 for bit in turning(count)) % 2


def turning(count):
    return sorted({0, max((count - 1).bit_length() - 1, 0)})


def gram_kernel(lines, scale, own, other, solved, piece):
    rows = own.shape[0] // 2
    half = own.shape[1] // 2
    section = lax.axis_index("sec")
    lead = section == 0
    first = jnp.where(lead, own[:rows, :], other[:rows, :])
    base = jnp.where(lead, other[:rows, :], own[:rows, :])
    carry = jnp.where(lead, other[rows:, :], own[rows:, :])
    firsts = terms(first, 2)
    second = base - product(terms(carry, 2), firsts, NN, 1)
    solved[...] = jnp.where(lead, first, second)
    seconds = terms(second, 2)
    gram = (product(firsts, firsts, TN, 1) + product(seconds, seconds, TN, 1)) * scale
    block, corner, diagonal = packed(gram, half)
    piece[:half, :] = jnp.where(section == turned(lines), block, corner)
    piece[half:, :] = jnp.broadcast_to(diagonal, (piece.shape[0] - half, half))


def eliminate(gram, inverse, factor):
    size = gram.shape[0]
    i, j = grids(size, size)
    inverse[...] = jnp.where(i == j, 1.0, 0.0)
    factor[...] = jnp.zeros_like(factor)
    lane = lax.broadcasted_iota(jnp.int32, (1, size), 1)
    line = lax.broadcasted_iota(jnp.int32, (size, 1), 0)

    def step(k, carry):
        matrix = gram[...]
        pivot = jnp.sum(jnp.where((i == k) & (j == k), matrix, 0.0), axis=(0, 1), keepdims=True)
        root = lax.rsqrt(pivot)
        root = root * (1.5 - 0.5 * pivot * root * root)
        column = jnp.sum(jnp.where(j == k, matrix, 0.0), axis=1, keepdims=True) * root
        row = jnp.sum(jnp.where(i == k, matrix, 0.0), axis=0, keepdims=True) * root
        row = jnp.where(lane >= k, row, 0.0)
        column = jnp.where(line > k, column, 0.0)
        lead = jnp.sum(jnp.where(i == k, inverse[...], 0.0), axis=0, keepdims=True) * root
        gram[...] = matrix - column * row
        inverse[...] = jnp.where(i == k, lead, inverse[...] - column * lead)
        factor[...] = jnp.where(i == k, row, factor[...])
        return carry

    lax.fori_loop(0, size, step, 0)


def improved(error, weight, unit):
    lower = error * weight
    return weight * coarse(lower, error) + (0.5 * unit * lower * lower - lower)


def factor_kernel(lines, mine, theirs, solved, panel, factor, gram_ref, inverse_ref, factor_ref, panel_ref, sems):
    half = mine.shape[1]
    size = 2 * half
    lead = lax.axis_index("sec") == turned(lines) if lines else True
    block = jnp.where(lead, mine[:half, :], theirs[:half, :])
    corner = jnp.where(lead, theirs[:half, :], mine[:half, :])
    diagonal = jnp.where(lead, theirs[half : half + 1, :], mine[half : half + 1, :])
    i, j = grids(half, half)
    mirrored = corner.T
    gram_ref[:half, :half] = jnp.where(i >= j, corner, mirrored)
    gram_ref[half:, half:] = jnp.where(i < j, corner, jnp.where(i == j, diagonal, mirrored))
    gram_ref[half:, :half] = block
    gram_ref[:half, half:] = block.T
    gram = gram_ref[...]

    i, j = grids(size, size)
    unit = jnp.where(i == j, 1.0, 0.0)
    weight = jnp.where(i > j, 1.0, jnp.where(i == j, 0.5, 0.0))
    spread = gram * unit
    row = lax.rsqrt(jnp.sum(spread, axis=0, keepdims=True))
    column = lax.rsqrt(jnp.sum(spread, axis=1, keepdims=True))
    scaled = gram * column * row
    scaleds = terms(scaled, 2)
    solveds = terms(solved[...] * row, 2)
    moves = [
        pltpu.make_async_copy(source, place, sems.at[k])
        for k, (source, place) in enumerate([(panel_ref, panel), (factor_ref, factor)])
    ]

    def attempt(trial):
        upper = product(trial, scaleds)
        near = product(solveds, trial, NT)
        error = product(terms(upper, 2), trial, NT) - unit
        step = terms(improved(error, weight, unit), 2)
        upper = upper + product(step, terms(upper, 2), NN, 1)
        factor_ref[...] = jnp.where(i <= j, upper / row, 0.0)
        moves[1].start()
        panel_ref[...] = near + product(terms(near, 2), step, NT, 1)
        moves[0].start()
        last = trial[0].astype(jnp.float32) + product(step, trial)
        error = product(terms(upper, 2), terms(last, 2), NT, 1) - unit
        open_entries = jnp.sum(jnp.where(jnp.abs(error) < 3e-5, 0.0, 1.0))
        moves[0].wait()
        moves[1].wait()
        return last, open_entries > 0.0

    trial = unit - (scaled - unit) * weight
    error = coarse(product(terms(trial, 1), scaleds[:1]), trial, NT) - unit
    trial = trial + coarse(improved(error, weight, unit), trial)
    trial, unsettled = attempt(terms(trial, 1))

    @pl.when(unsettled)
    def _():
        _, again = attempt(terms(trial, 1))

        @pl.when(again)
        def _():
            eliminate(gram_ref, inverse_ref, factor_ref)
            panel_ref[...] = exact(solved[...], inverse_ref[...], NT)
            for move in moves:
                move.start()
            for move in moves:
                move.wait()


def finish(lines, mine, theirs, solved):
    rows, size = solved.shape
    scratch = [pltpu.VMEM((size, size), jnp.float32)] * 3
    scratch += [pltpu.VMEM((rows, size), jnp.float32), pltpu.SemaphoreType.DMA((2,))]
    return call(
        functools.partial(factor_kernel, lines),
        [shape(rows, size), shape(size, size)],
        [VMEM, VMEM, VMEM],
        "factor",
        24 * 2 * size**3,
        scratch,
        HBM,
    )(mine, theirs, solved)


def paired(lines, masks):
    pairs = []
    for place in range(2 * lines):
        line, core = divmod(place, 2)
        odd = lambda value: sum(value >> bit & 1 for bit in turning(lines)) % 2
        mask = masks[core ^ odd(line)]
        pairs.append((place, place ^ 2 * mask ^ odd(mask)))
    return pairs


def swap_lines(piece, lines):
    bits = (lines - 1).bit_length()
    groups = [[2 << b, 1 << b, 3 << b] for b in range(0, bits - 1, 2)]
    turn = len(groups) // 2
    for one, two in zip(groups, groups[turn:] + groups[:turn]):
        a, b, c = (lax.ppermute(piece, AXES, paired(lines, masks)) for masks in zip(one, two))
        piece = (piece + a) + (b + c)
    if bits % 2:
        mask = 1 << bits - 1
        piece = piece + lax.ppermute(piece, AXES, paired(lines, (mask, mask)))
    return piece


def two_sections(target, inverse, coupled, links, lines):
    rows, width = target.shape
    half = width // 2
    own = call(
        front_kernel,
        [shape(rows + inverse.shape[0], width)],
        [HBM, HBM, HBM, HBM],
        "front",
        4 * rows * rows * width,
        [
            pltpu.SMEM(links.shape, jnp.int32),
            pltpu.VMEM(target.shape, jnp.float32),
            pltpu.VMEM(inverse.shape, jnp.float32),
            pltpu.VMEM(coupled.shape, jnp.float32),
            pltpu.SemaphoreType.DMA((4,)),
        ],
    )(*(fetched(x) for x in (links, target, inverse, coupled)))[0]
    swap = [(0, 1), (1, 0)]
    other = lax.ppermute(own, "sec", swap)
    scale = 1.0 / (2 * lines * rows)
    solved, piece = call(
        functools.partial(gram_kernel, lines, scale),
        [shape(rows, width), shape(half + 8, half)],
        [VMEM, VMEM],
        "gram",
        6 * rows * rows * width,
    )(own, other)
    piece = swap_lines(piece, lines)
    theirs = lax.ppermute(piece, "sec", swap)
    return finish(lines, piece, theirs, solved)


def many_sections(target, inverse, coupled, links):
    section = lax.axis_index("sec")
    count = lax.axis_size("sec")
    acc = target
    solved = jnp.zeros_like(target)
    for anchor in range(count):
        mine = section == anchor
        candidate = jnp.where(mine, highest(inverse, acc), 0.0)
        arrived = lax.psum(candidate, "sec")
        solved = jnp.where(mine, arrived, solved)
        matrix = jnp.zeros_like(inverse)
        for slot in range(coupled.shape[0]):
            matrix = matrix + jnp.where(links[slot] == anchor, coupled[slot], 0.0)
        acc = acc - highest(matrix, arrived)
    total = lax.axis_size("line") * count * target.shape[0]
    gram = lax.psum(highest(solved, solved, TN), AXES) / total
    half = target.shape[1] // 2
    block, corner, diagonal = packed(gram, half)
    rest = jnp.broadcast_to(diagonal, (8, half))
    return finish(0, jnp.concatenate([block, rest]), jnp.concatenate([corner, rest]), solved)


def shards(right_side, inverse_diag, couplings, neighbors):
    local = (right_side[0, 0], inverse_diag[0, 0], couplings[0, 0], neighbors[0, 0])
    lines = lax.axis_size("line")
    if lax.axis_size("sec") == 2 and lines & (lines - 1) == 0:
        panel, factor = two_sections(*local, lines)
    else:
        panel, factor = many_sections(*local)
    return (panel[None, None], factor)


def solution(mesh):
    placed = (
        P("line", "sec", None, None),
        P("line", "sec", None, None),
        P("line", "sec", None, None, None),
        P("line", "sec", None),
    )
    return jax.shard_map(
        shards,
        mesh=mesh,
        in_specs=placed,
        out_specs=(P("line", "sec", None, None), P()),
        check_vma=False,
    )
```

```python
import functools

import jax
import jax.numpy as jnp
from jax import lax
from jax.experimental import pallas as pl
from jax.experimental.pallas import tpu as pltpu
from jax.sharding import PartitionSpec as P


AXES = ("line", "sec")
VMEM = pl.BlockSpec(memory_space=pltpu.VMEM)
HBM = pl.BlockSpec(memory_space=pltpu.HBM)
NN = (((1,), (0,)), ((), ()))
NT = (((1,), (1,)), ((), ()))
TN = (((0,), (0,)), ((), ()))


def terms(value, count=3):
    parts = []
    for _ in range(count):
        parts.append(value.astype(jnp.bfloat16))
        value = value - parts[-1].astype(jnp.float32)
    return parts


def product(left, right, dims=NN, order=2):
    total = None
    for level in range(order, -1, -1):
        for i in range(len(left)):
            if 0 <= level - i < len(right):
                part = lax.dot_general(
                    left[i], right[level - i], dims, preferred_element_type=jnp.float32
                )
                total = part if total is None else total + part
    return total


def exact(left, right, dims=NN):
    return product(terms(left), terms(right), dims)


def coarse(left, right, dims=NN):
    return product(terms(left, 1), terms(right, 1), dims)


def highest(left, right, dims=NN):
    return lax.dot_general(
        left, right, dims, precision=lax.Precision.HIGHEST, preferred_element_type=jnp.float32
    )


def call(kernel, outs, specs, name, flops, scratch=(), place=VMEM):
    moved = sum(4 * out.size for out in outs)
    return pl.pallas_call(
        kernel,
        out_shape=outs,
        in_specs=specs,
        out_specs=[place] * len(outs),
        scratch_shapes=list(scratch),
        compiler_params=pltpu.CompilerParams(vmem_limit_bytes=16 << 20),
        cost_estimate=pl.CostEstimate(flops=flops, bytes_accessed=moved, transcendentals=0),
        name=name,
    )


def fetched(value):
    return pltpu.with_memory_space_constraint(value, pltpu.HBM)


def shape(*dims):
    return jax.ShapeDtypeStruct(dims, jnp.float32)


def grids(rows, cols):
    return (
        lax.broadcasted_iota(jnp.int32, (rows, cols), 0),
        lax.broadcasted_iota(jnp.int32, (rows, cols), 1),
    )


def front_kernel(links, target, inverse, coupled, out, chosen, right, left, blocks, sems):
    rows = right.shape[0]
    moves = [
        pltpu.make_async_copy(source, place, sems.at[k])
        for k, (source, place) in enumerate(
            [(inverse, left), (target, right), (links, chosen), (coupled, blocks)]
        )
    ]
    for move in moves:
        move.start()
    for move in moves:
        move.wait()
    matrix = jnp.zeros(left.shape, jnp.float32)
    for slot in range(blocks.shape[0]):
        matrix = matrix + jnp.where(chosen[slot] >= 0, blocks[slot], 0.0)
    both = jnp.concatenate([right[...], matrix], axis=1)
    both = product(terms(left[...], 2), terms(both, 2), NN, 1)
    out[:rows, :] = both[:, : right.shape[1]]
    out[rows:, :] = both[:, right.shape[1] :]


def packed(gram, half):
    i, j = grids(half, half)
    last = gram[half:, half:]
    corner = jnp.where(i >= j, gram[:half, :half], last)
    diagonal = jnp.sum(jnp.where(i == j, last, 0.0), axis=0, keepdims=True)
    return gram[half:, :half], corner, diagonal


def turned(count):
    line = lax.axis_index("line")
    return sum((line >> bit) & 1 for bit in turning(count)) % 2


def turning(count):
    return sorted({0, max((count - 1).bit_length() - 1, 0)})


def gram_kernel(lines, scale, own, other, solved, piece):
    rows = own.shape[0] // 2
    half = own.shape[1] // 2
    section = lax.axis_index("sec")
    lead = section == 0
    first = jnp.where(lead, own[:rows, :], other[:rows, :])
    base = jnp.where(lead, other[:rows, :], own[:rows, :])
    carry = jnp.where(lead, other[rows:, :], own[rows:, :])
    firsts = terms(first, 2)
    second = base - product(terms(carry, 2), firsts, NN, 1)
    solved[...] = jnp.where(lead, first, second)
    seconds = terms(second, 2)
    gram = product(firsts, firsts, TN, 1) + product(seconds, seconds, TN, 1)
    block, corner, diagonal = packed(gram, half)
    piece[:half, :] = jnp.where(section == turned(lines), block, corner) * scale
    piece[half:, :] = jnp.broadcast_to(diagonal * scale, (piece.shape[0] - half, half))


def eliminate(gram, inverse, factor):
    size = gram.shape[0]
    i, j = grids(size, size)
    inverse[...] = jnp.where(i == j, 1.0, 0.0)
    factor[...] = jnp.zeros_like(factor)
    lane = lax.broadcasted_iota(jnp.int32, (1, size), 1)
    line = lax.broadcasted_iota(jnp.int32, (size, 1), 0)

    def step(k, carry):
        matrix = gram[...]
        pivot = jnp.sum(jnp.where((i == k) & (j == k), matrix, 0.0), axis=(0, 1), keepdims=True)
        root = lax.rsqrt(pivot)
        root = root * (1.5 - 0.5 * pivot * root * root)
        column = jnp.sum(jnp.where(j == k, matrix, 0.0), axis=1, keepdims=True) * root
        row = jnp.sum(jnp.where(i == k, matrix, 0.0), axis=0, keepdims=True) * root
        row = jnp.where(lane >= k, row, 0.0)
        column = jnp.where(line > k, column, 0.0)
        lead = jnp.sum(jnp.where(i == k, inverse[...], 0.0), axis=0, keepdims=True) * root
        gram[...] = matrix - column * row
        inverse[...] = jnp.where(i == k, lead, inverse[...] - column * lead)
        factor[...] = jnp.where(i == k, row, factor[...])
        return carry

    lax.fori_loop(0, size, step, 0)


def improved(error, weight, unit):
    lower = error * weight
    return weight * coarse(lower, error) + (0.5 * unit * lower * lower - lower)


def factor_kernel(lines, mine, theirs, solved, panel, factor, gram_ref, inverse_ref, factor_ref, panel_ref, sems):
    half = mine.shape[1]
    size = 2 * half
    lead = lax.axis_index("sec") == turned(lines) if lines else True
    block = jnp.where(lead, mine[:half, :], theirs[:half, :])
    corner = jnp.where(lead, theirs[:half, :], mine[:half, :])
    diagonal = jnp.where(lead, theirs[half : half + 1, :], mine[half : half + 1, :])
    i, j = grids(half, half)
    mirrored = corner.T
    gram_ref[:half, :half] = jnp.where(i >= j, corner, mirrored)
    gram_ref[half:, half:] = jnp.where(i < j, corner, jnp.where(i == j, diagonal, mirrored))
    gram_ref[half:, :half] = block
    gram_ref[:half, half:] = block.T
    gram = gram_ref[...]

    i, j = grids(size, size)
    unit = jnp.where(i == j, 1.0, 0.0)
    weight = jnp.where(i > j, 1.0, jnp.where(i == j, 0.5, 0.0))
    spread = gram * unit
    row = lax.rsqrt(jnp.sum(spread, axis=0, keepdims=True))
    column = lax.rsqrt(jnp.sum(spread, axis=1, keepdims=True))
    scaled = gram * column * row
    scaleds = terms(scaled, 2)
    solveds = terms(solved[...] * row, 2)
    moves = [
        pltpu.make_async_copy(source, place, sems.at[k])
        for k, (source, place) in enumerate([(panel_ref, panel), (factor_ref, factor)])
    ]

    def attempt(trial):
        upper = product(trial, scaleds)
        near = product(solveds, trial, NT)
        error = product(terms(upper, 2), trial, NT) - unit
        step = terms(improved(error, weight, unit), 2)
        upper = upper + product(step, terms(upper, 2), NN, 1)
        factor_ref[...] = jnp.where(i <= j, upper / row, 0.0)
        moves[1].start()
        panel_ref[...] = near + product(terms(near, 2), step, NT, 1)
        moves[0].start()
        last = trial[0].astype(jnp.float32) + product(step, trial)
        error = product(terms(upper, 2), terms(last, 2), NT, 1) - unit
        open_entries = jnp.sum(jnp.where(jnp.abs(error) < 3e-5, 0.0, 1.0))
        moves[0].wait()
        moves[1].wait()
        return last, open_entries > 0.0

    trial = unit - (scaled - unit) * weight
    error = coarse(product(terms(trial, 1), scaleds[:1]), trial, NT) - unit
    trial = trial + coarse(improved(error, weight, unit), trial)
    trial, unsettled = attempt(terms(trial, 1))

    @pl.when(unsettled)
    def _():
        _, again = attempt(terms(trial, 1))

        @pl.when(again)
        def _():
            eliminate(gram_ref, inverse_ref, factor_ref)
            panel_ref[...] = exact(solved[...], inverse_ref[...], NT)
            for move in moves:
                move.start()
            for move in moves:
                move.wait()


def finish(lines, mine, theirs, solved):
    rows, size = solved.shape
    scratch = [pltpu.VMEM((size, size), jnp.float32)] * 3
    scratch += [pltpu.VMEM((rows, size), jnp.float32), pltpu.SemaphoreType.DMA((2,))]
    return call(
        functools.partial(factor_kernel, lines),
        [shape(rows, size), shape(size, size)],
        [VMEM, VMEM, VMEM],
        "factor",
        24 * 2 * size**3,
        scratch,
        HBM,
    )(mine, theirs, solved)


def paired(lines, masks):
    pairs = []
    for place in range(2 * lines):
        line, core = divmod(place, 2)
        odd = lambda value: sum(value >> bit & 1 for bit in turning(lines)) % 2
        mask = masks[core ^ odd(line)]
        pairs.append((place, place ^ 2 * mask ^ odd(mask)))
    return pairs


def swap_lines(piece, lines):
    bits = (lines - 1).bit_length()
    groups = [[2 << b, 1 << b, 3 << b] for b in range(0, bits - 1, 2)]
    turn = len(groups) // 2
    for one, two in zip(groups, groups[turn:] + groups[:turn]):
        a, b, c = (lax.ppermute(piece, AXES, paired(lines, masks)) for masks in zip(one, two))
        piece = (piece + a) + (b + c)
    if bits % 2:
        mask = 1 << bits - 1
        piece = piece + lax.ppermute(piece, AXES, paired(lines, (mask, mask)))
    return piece


def two_sections(target, inverse, coupled, links, lines):
    rows, width = target.shape
    half = width // 2
    own = call(
        front_kernel,
        [shape(rows + inverse.shape[0], width)],
        [HBM, HBM, HBM, HBM],
        "front",
        4 * rows * rows * width,
        [
            pltpu.SMEM(links.shape, jnp.int32),
            pltpu.VMEM(target.shape, jnp.float32),
            pltpu.VMEM(inverse.shape, jnp.float32),
            pltpu.VMEM(coupled.shape, jnp.float32),
            pltpu.SemaphoreType.DMA((4,)),
        ],
    )(*(fetched(x) for x in (links, target, inverse, coupled)))[0]
    swap = [(0, 1), (1, 0)]
    other = lax.ppermute(own, "sec", swap)
    scale = 1.0 / (2 * lines * rows)
    solved, piece = call(
        functools.partial(gram_kernel, lines, scale),
        [shape(rows, width), shape(half + 8, half)],
        [VMEM, VMEM],
        "gram",
        6 * rows * rows * width,
    )(own, other)
    piece = swap_lines(piece, lines)
    theirs = lax.ppermute(piece, "sec", swap)
    return finish(lines, piece, theirs, solved)


def many_sections(target, inverse, coupled, links):
    section = lax.axis_index("sec")
    count = lax.axis_size("sec")
    acc = target
    solved = jnp.zeros_like(target)
    for anchor in range(count):
        mine = section == anchor
        candidate = jnp.where(mine, highest(inverse, acc), 0.0)
        arrived = lax.psum(candidate, "sec")
        solved = jnp.where(mine, arrived, solved)
        matrix = jnp.zeros_like(inverse)
        for slot in range(coupled.shape[0]):
            matrix = matrix + jnp.where(links[slot] == anchor, coupled[slot], 0.0)
        acc = acc - highest(matrix, arrived)
    total = lax.axis_size("line") * count * target.shape[0]
    gram = lax.psum(highest(solved, solved, TN), AXES) / total
    half = target.shape[1] // 2
    block, corner, diagonal = packed(gram, half)
    rest = jnp.broadcast_to(diagonal, (8, half))
    return finish(0, jnp.concatenate([block, rest]), jnp.concatenate([corner, rest]), solved)


def shards(right_side, inverse_diag, couplings, neighbors):
    local = (right_side[0, 0], inverse_diag[0, 0], couplings[0, 0], neighbors[0, 0])
    lines = lax.axis_size("line")
    if lax.axis_size("sec") == 2 and lines & (lines - 1) == 0:
        panel, factor = two_sections(*local, lines)
    else:
        panel, factor = many_sections(*local)
    return (panel[None, None], factor)


def solution(mesh):
    placed = (
        P("line", "sec", None, None),
        P("line", "sec", None, None),
        P("line", "sec", None, None, None),
        P("line", "sec", None),
    )
    return jax.shard_map(
        shards,
        mesh=mesh,
        in_specs=placed,
        out_specs=(P("line", "sec", None, None), P()),
        check_vma=False,
    )
```

```python
import functools

import jax
import jax.numpy as jnp
from jax import lax
from jax.experimental import pallas as pl
from jax.experimental.pallas import tpu as pltpu
from jax.sharding import PartitionSpec as P


AXES = ("line", "sec")
VMEM = pl.BlockSpec(memory_space=pltpu.VMEM)
HBM = pl.BlockSpec(memory_space=pltpu.HBM)
NN = (((1,), (0,)), ((), ()))
NT = (((1,), (1,)), ((), ()))
TN = (((0,), (0,)), ((), ()))


def terms(value, count=3):
    parts = []
    for _ in range(count):
        parts.append(value.astype(jnp.bfloat16))
        value = value - parts[-1].astype(jnp.float32)
    return parts


def product(left, right, dims=NN, order=2):
    total = None
    for level in range(order, -1, -1):
        for i in range(len(left)):
            if 0 <= level - i < len(right):
                part = lax.dot_general(
                    left[i], right[level - i], dims, preferred_element_type=jnp.float32
                )
                total = part if total is None else total + part
    return total


def exact(left, right, dims=NN):
    return product(terms(left), terms(right), dims)


def coarse(left, right, dims=NN):
    return product(terms(left, 1), terms(right, 1), dims)


def highest(left, right, dims=NN):
    return lax.dot_general(
        left, right, dims, precision=lax.Precision.HIGHEST, preferred_element_type=jnp.float32
    )


def call(kernel, outs, specs, name, flops, scratch=(), place=VMEM):
    moved = sum(4 * out.size for out in outs)
    return pl.pallas_call(
        kernel,
        out_shape=outs,
        in_specs=specs,
        out_specs=[place] * len(outs),
        scratch_shapes=list(scratch),
        compiler_params=pltpu.CompilerParams(vmem_limit_bytes=16 << 20),
        cost_estimate=pl.CostEstimate(flops=flops, bytes_accessed=moved, transcendentals=0),
        name=name,
    )


def fetched(value):
    return pltpu.with_memory_space_constraint(value, pltpu.HBM)


def shape(*dims):
    return jax.ShapeDtypeStruct(dims, jnp.float32)


def grids(rows, cols):
    return (
        lax.broadcasted_iota(jnp.int32, (rows, cols), 0),
        lax.broadcasted_iota(jnp.int32, (rows, cols), 1),
    )


def front_kernel(links, target, inverse, coupled, out, chosen, right, left, blocks, sems):
    rows = right.shape[0]
    moves = [
        pltpu.make_async_copy(source, place, sems.at[k])
        for k, (source, place) in enumerate(
            [(inverse, left), (target, right), (links, chosen), (coupled, blocks)]
        )
    ]
    for move in moves:
        move.start()
    for move in moves:
        move.wait()
    matrix = jnp.zeros(left.shape, jnp.float32)
    for slot in range(blocks.shape[0]):
        matrix = matrix + jnp.where(chosen[slot] >= 0, blocks[slot], 0.0)
    both = jnp.concatenate([right[...], matrix], axis=1)
    both = product(terms(left[...], 2), terms(both, 2), NN, 1)
    out[:rows, :] = both[:, : right.shape[1]]
    out[rows:, :] = both[:, right.shape[1] :]


def packed(gram, half):
    i, j = grids(half, half)
    last = gram[half:, half:]
    corner = jnp.where(i >= j, gram[:half, :half], last)
    diagonal = jnp.sum(jnp.where(i == j, last, 0.0), axis=0, keepdims=True)
    return gram[half:, :half], corner, diagonal


def turned(count):
    line = lax.axis_index("line")
    return sum((line >> bit) & 1 for bit in turning(count)) % 2


def turning(count):
    return sorted({0, max((count - 1).bit_length() - 1, 0)})


def gram_kernel(lines, scale, own, other, solved, piece):
    rows = own.shape[0] // 2
    half = own.shape[1] // 2
    section = lax.axis_index("sec")
    lead = section == 0
    first = jnp.where(lead, own[:rows, :], other[:rows, :])
    base = jnp.where(lead, other[:rows, :], own[:rows, :])
    carry = jnp.where(lead, other[rows:, :], own[rows:, :])
    firsts = terms(first, 2)
    second = base - product(terms(carry, 2), firsts, NN, 1)
    solved[...] = jnp.where(lead, first, second)
    seconds = terms(second, 2)
    gram = product(firsts, firsts, TN, 1) + product(seconds, seconds, TN, 1)
    block, corner, diagonal = packed(gram, half)
    piece[:half, :] = jnp.where(section == turned(lines), block, corner) * scale
    piece[half:, :] = jnp.broadcast_to(diagonal * scale, (piece.shape[0] - half, half))


def eliminate(gram, inverse, factor):
    size = gram.shape[0]
    i, j = grids(size, size)
    inverse[...] = jnp.where(i == j, 1.0, 0.0)
    factor[...] = jnp.zeros_like(factor)
    lane = lax.broadcasted_iota(jnp.int32, (1, size), 1)
    line = lax.broadcasted_iota(jnp.int32, (size, 1), 0)

    def step(k, carry):
        matrix = gram[...]
        pivot = jnp.sum(jnp.where((i == k) & (j == k), matrix, 0.0), axis=(0, 1), keepdims=True)
        root = lax.rsqrt(pivot)
        root = root * (1.5 - 0.5 * pivot * root * root)
        column = jnp.sum(jnp.where(j == k, matrix, 0.0), axis=1, keepdims=True) * root
        row = jnp.sum(jnp.where(i == k, matrix, 0.0), axis=0, keepdims=True) * root
        row = jnp.where(lane >= k, row, 0.0)
        column = jnp.where(line > k, column, 0.0)
        lead = jnp.sum(jnp.where(i == k, inverse[...], 0.0), axis=0, keepdims=True) * root
        gram[...] = matrix - column * row
        inverse[...] = jnp.where(i == k, lead, inverse[...] - column * lead)
        factor[...] = jnp.where(i == k, row, factor[...])
        return carry

    lax.fori_loop(0, size, step, 0)


def improved(error, weight, unit):
    lower = error * weight
    return weight * coarse(lower, error) + (0.5 * unit * lower * lower - lower)


def factor_kernel(lines, mine, theirs, solved, panel, factor, gram_ref, inverse_ref, factor_ref, panel_ref, sems):
    half = mine.shape[1]
    size = 2 * half
    lead = lax.axis_index("sec") == turned(lines) if lines else True
    block = jnp.where(lead, mine[:half, :], theirs[:half, :])
    corner = jnp.where(lead, theirs[:half, :], mine[:half, :])
    diagonal = jnp.where(lead, theirs[half : half + 1, :], mine[half : half + 1, :])
    i, j = grids(half, half)
    mirrored = corner.T
    gram_ref[:half, :half] = jnp.where(i >= j, corner, mirrored)
    gram_ref[half:, half:] = jnp.where(i < j, corner, jnp.where(i == j, diagonal, mirrored))
    gram_ref[half:, :half] = block
    gram_ref[:half, half:] = block.T
    gram = gram_ref[...]

    i, j = grids(size, size)
    unit = jnp.where(i == j, 1.0, 0.0)
    weight = jnp.where(i > j, 1.0, jnp.where(i == j, 0.5, 0.0))
    spread = gram * unit
    power = jnp.sum(spread, axis=0, keepdims=True)
    row = lax.rsqrt(power)
    root = row * power
    column = lax.rsqrt(jnp.sum(spread, axis=1, keepdims=True))
    scaled = gram * column * row
    scaleds = terms(scaled, 2)
    solveds = terms(solved[...] * row, 2)
    moves = [
        pltpu.make_async_copy(source, place, sems.at[k])
        for k, (source, place) in enumerate([(panel_ref, panel), (factor_ref, factor)])
    ]

    def attempt(trial):
        upper = product(trial, scaleds)
        near = product(solveds, trial, NT)
        error = product(terms(upper, 2), trial, NT) - unit
        step = terms(improved(error, weight, unit), 2)
        upper = upper + product(step, terms(upper, 2), NN, 1)
        factor_ref[...] = jnp.where(i <= j, upper * root, 0.0)
        moves[1].start()
        panel_ref[...] = near + product(terms(near, 2), step, NT, 1)
        moves[0].start()
        last = trial[0].astype(jnp.float32) + product(step, trial)
        error = product(terms(upper, 2), terms(last, 2), NT, 1) - unit
        open_entries = jnp.sum(jnp.where(jnp.abs(error) < 3e-5, 0.0, 1.0))
        moves[0].wait()
        moves[1].wait()
        return last, open_entries > 0.0

    trial = unit - (scaled - unit) * weight
    error = coarse(product(terms(trial, 1), scaleds[:1]), trial, NT) - unit
    trial = trial + coarse(improved(error, weight, unit), trial)
    trial, unsettled = attempt(terms(trial, 1))

    @pl.when(unsettled)
    def _():
        _, again = attempt(terms(trial, 1))

        @pl.when(again)
        def _():
            eliminate(gram_ref, inverse_ref, factor_ref)
            panel_ref[...] = exact(solved[...], inverse_ref[...], NT)
            for move in moves:
                move.start()
            for move in moves:
                move.wait()


def finish(lines, mine, theirs, solved):
    rows, size = solved.shape
    scratch = [pltpu.VMEM((size, size), jnp.float32)] * 3
    scratch += [pltpu.VMEM((rows, size), jnp.float32), pltpu.SemaphoreType.DMA((2,))]
    return call(
        functools.partial(factor_kernel, lines),
        [shape(rows, size), shape(size, size)],
        [VMEM, VMEM, VMEM],
        "factor",
        24 * 2 * size**3,
        scratch,
        HBM,
    )(mine, theirs, solved)


def paired(lines, masks):
    pairs = []
    for place in range(2 * lines):
        line, core = divmod(place, 2)
        odd = lambda value: sum(value >> bit & 1 for bit in turning(lines)) % 2
        mask = masks[core ^ odd(line)]
        pairs.append((place, place ^ 2 * mask ^ odd(mask)))
    return pairs


def swap_lines(piece, lines):
    bits = (lines - 1).bit_length()
    groups = [[2 << b, 1 << b, 3 << b] for b in range(0, bits - 1, 2)]
    turn = len(groups) // 2
    for one, two in zip(groups, groups[turn:] + groups[:turn]):
        a, b, c = (lax.ppermute(piece, AXES, paired(lines, masks)) for masks in zip(one, two))
        piece = (piece + a) + (b + c)
    if bits % 2:
        mask = 1 << bits - 1
        piece = piece + lax.ppermute(piece, AXES, paired(lines, (mask, mask)))
    return piece


def two_sections(target, inverse, coupled, links, lines):
    rows, width = target.shape
    half = width // 2
    own = call(
        front_kernel,
        [shape(rows + inverse.shape[0], width)],
        [HBM, HBM, HBM, HBM],
        "front",
        4 * rows * rows * width,
        [
            pltpu.SMEM(links.shape, jnp.int32),
            pltpu.VMEM(target.shape, jnp.float32),
            pltpu.VMEM(inverse.shape, jnp.float32),
            pltpu.VMEM(coupled.shape, jnp.float32),
            pltpu.SemaphoreType.DMA((4,)),
        ],
    )(*(fetched(x) for x in (links, target, inverse, coupled)))[0]
    swap = [(0, 1), (1, 0)]
    other = lax.ppermute(own, "sec", swap)
    scale = 1.0 / (2 * lines * rows)
    solved, piece = call(
        functools.partial(gram_kernel, lines, scale),
        [shape(rows, width), shape(half + 8, half)],
        [VMEM, VMEM],
        "gram",
        6 * rows * rows * width,
    )(own, other)
    piece = swap_lines(piece, lines)
    theirs = lax.ppermute(piece, "sec", swap)
    return finish(lines, piece, theirs, solved)


def many_sections(target, inverse, coupled, links):
    section = lax.axis_index("sec")
    count = lax.axis_size("sec")
    acc = target
    solved = jnp.zeros_like(target)
    for anchor in range(count):
        mine = section == anchor
        candidate = jnp.where(mine, highest(inverse, acc), 0.0)
        arrived = lax.psum(candidate, "sec")
        solved = jnp.where(mine, arrived, solved)
        matrix = jnp.zeros_like(inverse)
        for slot in range(coupled.shape[0]):
            matrix = matrix + jnp.where(links[slot] == anchor, coupled[slot], 0.0)
        acc = acc - highest(matrix, arrived)
    total = lax.axis_size("line") * count * target.shape[0]
    gram = lax.psum(highest(solved, solved, TN), AXES) / total
    half = target.shape[1] // 2
    block, corner, diagonal = packed(gram, half)
    rest = jnp.broadcast_to(diagonal, (8, half))
    return finish(0, jnp.concatenate([block, rest]), jnp.concatenate([corner, rest]), solved)


def shards(right_side, inverse_diag, couplings, neighbors):
    local = (right_side[0, 0], inverse_diag[0, 0], couplings[0, 0], neighbors[0, 0])
    lines = lax.axis_size("line")
    if lax.axis_size("sec") == 2 and lines & (lines - 1) == 0:
        panel, factor = two_sections(*local, lines)
    else:
        panel, factor = many_sections(*local)
    return (panel[None, None], factor)


def solution(mesh):
    placed = (
        P("line", "sec", None, None),
        P("line", "sec", None, None),
        P("line", "sec", None, None, None),
        P("line", "sec", None),
    )
    return jax.shard_map(
        shards,
        mesh=mesh,
        in_specs=placed,
        out_specs=(P("line", "sec", None, None), P()),
        check_vma=False,
    )
```
